256 devices in a mesh: section: 32 (over x_hi, z, core), expert: 8 (over x_lo, y).
Axes of the slice: x: 4 (x_hi: 2, x_lo: 2; x = x_hi * 2 + x_lo), y: 4, z: 8, core: 2. Of those that a mesh axis runs over, the one named last changes fastest.
Arguments:
- tokens: bfloat16 [1536, 6144], P('expert', 'section'), may hold values from -6 to 6
- expert_ids: int32 [1536, 2], P('expert'), may hold values from 0 to 7, as said below
- slot_ids: int32 [1536, 2], P('expert'), may hold values from 0 to 47, as said below
- router: float32 [6144, 8], replicated, may hold values from -0.078125 to 0.078125
- up_weight: bfloat16 [8, 6144, 8192], P('expert', None, 'section'), may hold values from -0.078125 to 0.078125
- down_weight: bfloat16 [8, 8192, 6144], P('expert', 'section'), may hold values from -0.0625 to 0.0625
- cotangent: bfloat16 [1536, 6144], P('expert', 'section'), may hold values from -6 to 6
Outputs:
- mixed: bfloat16 [1536, 6144], P('expert', 'section')
- grad_tokens: bfloat16 [1536, 6144], P('expert', 'section')
- grad_up: bfloat16 [8, 6144, 8192], P('expert', None, 'section')
- grad_down: bfloat16 [8, 8192, 6144], P('expert', 'section')
- grad_router: float32 [6144, 8], replicated
The draws below stay inside these ranges and needn't reach their ends.
Inputs may be any that keep to these rules, and one draw needn't show every extreme that they name: `expert_ids`: within each block of 192 consecutive tokens (one group), a token's two experts differ and every expert is chosen exactly 48 times. `slot_ids`: within each block of 192 consecutive tokens, the 48 choices of one expert take the slots 0 to 47 once each.
All inputs are finite; a program needn't handle non-finite values.
Results may differ from the reference program's by a relative error of at most 0.019.
Values may be sent and summed in bfloat16 or wider, within the bound.
A program may use at most 128 MiB of HBM per device.

```python
import jax
import jax.numpy as jnp
from jax import lax

D = 6144
FF_WIN = 8192
TOK_DEV = 192
EXPERTS = 8
CAP = 48
TOKENS = 1536
N_SECTION = 32


def routing_table(key):
    base = jax.random.fold_in(key, 1234)
    block_keys = jax.random.split(base, TOKENS // TOK_DEV)

    def block_route(block_key):
        label_key, order_key, flip_key = jax.random.split(block_key, 3)
        relabel = jax.random.permutation(label_key, EXPERTS).astype(jnp.int32)
        ordering = jax.random.permutation(order_key, TOK_DEV).astype(jnp.int32)
        flipped = jax.random.randint(flip_key, (TOK_DEV,), 0, 2, dtype=jnp.int32)
        first = 2 * ordering + flipped
        second = 2 * ordering + 1 - flipped
        pair_index = jnp.stack([first, second], axis=1)
        return (relabel[pair_index % EXPERTS], pair_index // EXPERTS)
    chosen, placed = jax.vmap(block_route)(block_keys)
    return (chosen.reshape(TOKENS, 2).astype(jnp.int32), placed.reshape(TOKENS, 2).astype(jnp.int32))


def draw_expert_ids(key, part):
    return routing_table(key)[0]


def draw_slot_ids(key, part):
    return routing_table(key)[1]


def levels(rng, dims, cuts, least, high):
    factor_of, own = 1.0, jax.random.fold_in(rng, 6)
    for axis_at, shards_of in cuts:
        heights = jnp.exp(jax.random.uniform(jax.random.fold_in(own, axis_at), (shards_of,), jnp.float32, least / len(cuts), high / len(cuts)))
        factor_of = factor_of * jnp.repeat(heights, dims[axis_at] // shards_of).reshape([-1 if axis == axis_at else 1 for axis in range(len(dims))])
    return factor_of


def normal_values(rng, extent, deviation, reach, shards=(), held_as=jnp.bfloat16):
    result = deviation * jax.random.normal(rng, extent, jnp.float32)
    if shards:
        result = result * levels(rng, extent, shards, -0.22, 0.18)
    return jnp.clip(result, -reach, reach).astype(held_as)


def setup_inputs(seed: int = 0) -> dict:
    splits = jax.random.split(jax.random.key(seed), 8)
    tokens = normal_values(splits[0], (TOKENS, D), 1.0, 6.0, ((0, 8), (1, 32)))
    expert_ids = draw_expert_ids(jax.random.fold_in(splits[7], 71), 0)
    slot_ids = draw_slot_ids(jax.random.fold_in(splits[7], 71), 0)
    router = normal_values(splits[3], (D, EXPERTS), D ** -0.5, 0.078125, (), jnp.float32)
    up_weight = normal_values(splits[4], (EXPERTS, D, FF_WIN), D ** -0.5, 0.078125, ((0, 8), (2, 32)))
    down_weight = normal_values(splits[5], (EXPERTS, FF_WIN, D), FF_WIN ** -0.5, 0.0625, ((0, 8), (1, 32)))
    cotangent = normal_values(splits[6], (TOKENS, D), 1.0, 6.0, ((0, 8), (1, 32)))
    return {"tokens": tokens, "expert_ids": expert_ids, "slot_ids": slot_ids, "router": router, "up_weight": up_weight, "down_weight": down_weight, "cotangent": cotangent}


def reference(tokens, expert_ids, slot_ids, router, up_weight, down_weight, cotangent):
    token_count, model_width = tokens.shape
    n_expert = router.shape[1]
    rows_expert = (token_count // TOK_DEV) * CAP
    block_width = FF_WIN // N_SECTION
    logits = jnp.dot(tokens.astype(jnp.float32), router, precision=lax.Precision.HIGHEST)
    picked = jnp.take_along_axis(logits, expert_ids, axis=1)
    logit_gap = picked[:, 0] - picked[:, 1]
    gate_first = jax.nn.sigmoid(logit_gap)
    gate_second = jax.nn.sigmoid(-logit_gap)
    gate_pair = jnp.stack([gate_first, gate_second], axis=1)
    group = (jnp.arange(token_count, dtype=jnp.int32) // TOK_DEV).astype(jnp.int32)
    target = (expert_ids * rows_expert + group[:, None] * CAP + slot_ids).astype(jnp.int32)
    flat_target = target.reshape(-1)
    sent_rows = jnp.repeat(tokens, 2, axis=0)
    dispatched = jnp.zeros((n_expert * rows_expert, model_width), jnp.bfloat16).at[flat_target].set(sent_rows)
    scaled = (cotangent.astype(jnp.float32)[:, None, :] * gate_pair[:, :, None]).astype(jnp.bfloat16)
    cot_rows = jnp.zeros((n_expert * rows_expert, model_width), jnp.bfloat16).at[flat_target].set(scaled.reshape(-1, model_width))
    dispatched = dispatched.reshape(n_expert, rows_expert, model_width)
    cot_rows = cot_rows.reshape(n_expert, rows_expert, model_width)

    def expert_pass(operands):
        rows_in, rows_cot, weight_in, weight_out = operands
        pre_act = jnp.dot(rows_in, weight_in, preferred_element_type=jnp.float32)
        sigma = jax.nn.sigmoid(pre_act)
        hidden = (pre_act * sigma).astype(jnp.bfloat16)
        hidden_grad = jnp.dot(rows_cot, weight_out.T, preferred_element_type=jnp.float32)
        pre_grad = (hidden_grad * sigma * (1.0 + pre_act * (1.0 - sigma))).astype(jnp.bfloat16)
        grad_out_weight = jnp.dot(hidden.T, rows_cot, preferred_element_type=jnp.float32).astype(jnp.bfloat16)
        grad_in_weight = jnp.dot(rows_in.T, pre_grad, preferred_element_type=jnp.float32).astype(jnp.bfloat16)

        def block_step(carry, block):
            start = (block * block_width).astype(jnp.int32)
            hid_block = lax.dynamic_slice_in_dim(hidden, start, block_width, 1)
            grad_block = lax.dynamic_slice_in_dim(pre_grad, start, block_width, 1)
            out_block = lax.dynamic_slice_in_dim(weight_out, start, block_width, 0)
            in_block = lax.dynamic_slice_in_dim(weight_in, start, block_width, 1)
            forward_part = jnp.dot(hid_block, out_block, preferred_element_type=jnp.float32).astype(jnp.bfloat16)
            backward_part = lax.dot_general(grad_block, in_block, (((1,), (1,)), ((), ())), preferred_element_type=jnp.float32).astype(jnp.bfloat16)
            forward_part, backward_part = lax.optimization_barrier((forward_part, backward_part))
            return (carry[0] + forward_part.astype(jnp.float32), carry[1] + backward_part.astype(jnp.float32)), None

        zeros_rows = jnp.zeros((rows_expert, model_width), jnp.float32)
        sums_pair, unused = lax.scan(block_step, (zeros_rows, zeros_rows), jnp.arange(N_SECTION, dtype=jnp.int32))
        return sums_pair[0].astype(jnp.bfloat16), sums_pair[1].astype(jnp.bfloat16), grad_in_weight, grad_out_weight

    expert_out, expert_back, grad_up, grad_down = lax.map(expert_pass, (dispatched, cot_rows, up_weight, down_weight))
    flat_out = expert_out.reshape(-1, model_width)
    flat_back = expert_back.reshape(-1, model_width)
    taken = flat_out[target].astype(jnp.float32)
    taken_back = flat_back[target].astype(jnp.float32)
    mixed = gate_pair[:, 0:1] * taken[:, 0] + gate_pair[:, 1:2] * taken[:, 1]
    gate_grad = jnp.sum(cotangent.astype(jnp.float32)[:, None, :] * taken, axis=2)
    logit_grad = (gate_grad[:, 0] - gate_grad[:, 1]) * gate_first * gate_second
    choose = (expert_ids[:, :, None] == jnp.arange(n_expert, dtype=jnp.int32)[None, None, :]).astype(jnp.float32)
    logits_grad = (choose[:, 0, :] - choose[:, 1, :]) * logit_grad[:, None]
    grad_tokens = taken_back[:, 0] + taken_back[:, 1] + jnp.dot(logits_grad, router.T, precision=lax.Precision.HIGHEST)
    grad_router = jnp.dot(tokens.astype(jnp.float32).T, logits_grad, precision=lax.Precision.HIGHEST)
    return mixed.astype(jnp.bfloat16), grad_tokens.astype(jnp.bfloat16), grad_up, grad_down, grad_router
```

```python
import jax
import jax.numpy as jnp
from jax import lax
from jax.experimental import pallas as pl
from jax.experimental.pallas import tpu as pltpu
from jax.sharding import PartitionSpec as P

MESH = pl.DeviceIdType.MESH
NZ = 8
FAR = NZ // 2
NE = 8
CAP = 48
TOK = 192
FEAT = 192
BLK = 2 * FEAT
ROWS = NE * CAP
HALF = ROWS // 2
QUART = HALF // 2
HID = 256
WIDTH = 6144
NBLK = WIDTH // BLK
BF = jnp.bfloat16
F32 = jnp.float32
LO = pl.ds(0, HALF)
HI = pl.ds(HALF, HALF)


def dot_nn(a, b):
    return jnp.dot(a, b, preferred_element_type=F32)


def dot_nt(a, b):
    return lax.dot_general(a, b, (((1,), (1,)), ((), ())), preferred_element_type=F32)


def dot_tn(a, b):
    return lax.dot_general(a, b, (((0,), (0,)), ((), ())), preferred_element_type=F32)


def lanes(p):
    return pl.ds(pl.multiple_of(p * BLK, BLK), BLK)


def rows_of(q):
    return pl.ds(pl.multiple_of(q * CAP, CAP), CAP)


def kernel(
    keep_ref, give_ref, ids_ref, slots_ref, rt_ref, up_ref, dn_ref,
    om_ref, og_ref, gu_ref, gd_ref, gr_ref,
    gath, wu, wd, gu, gd, rt3, pick, xch, sent, msend, meta,
    pre, logit, ms, mr, pg, tsb, tlb, part,
    ta_s, ta_r, tb_s, tb_r, tp_s, tp_r, xs, xr,
    fs0, fs1, ret0, ret1, outs, outr,
    gp, g1, g2s, g2, g3s, g3,
    w_sem, x_sem, d_ssem, d_rsem, m_ssem, m_rsem,
    a_ssem, a_rsem, b_ssem, b_rsem, p_ssem, p_rsem, f_ssem, f_rsem,
    mid_sem, ra_ssem, ra_rsem, rb_ssem, rb_rsem, rp_ssem, rp_rsem, rx_ssem, rx_rsem,
    gsem, r_ssem, r_rsem, q_ssem, q_rsem, o_sem,
    g1_ssem, g1_rsem, g2_ssem, g2_rsem, g3_ssem, g3_rsem, g4_sem,
):
    s = lax.axis_index("section")
    q = lax.axis_index("expert")
    c = lax.rem(s, 2)
    z = lax.rem(s // 2, NZ)
    h = s // (2 * NZ)

    def dev(hh, zz, cc, qq):
        return ((hh * NZ + zz) * 2 + cc, qq)

    def zwrap(v):
        return lax.rem(v + 2 * NZ, NZ)

    def qwrap(v):
        return lax.rem(v + NE, NE)

    sib = dev(h, z, 1 - c, q)
    partner = dev(1 - h, z, c, q)
    zdev = (dev(h, zwrap(z + 1), c, q), dev(h, zwrap(z - 1), c, q))

    def znext(d):
        return dev(h, zwrap(z + 1 - 2 * d), c, q)

    def rcopy(src, dst, ssem, rsem, target):
        return pltpu.make_async_remote_copy(
            src_ref=src, dst_ref=dst, send_sem=ssem, recv_sem=rsem, device_id=target, device_id_type=MESH
        )

    barrier = pltpu.get_barrier_semaphore()
    peers = [sib]
    for dh in range(2):
        for dq in range(NE):
            if dh or dq:
                peers.append(dev(lax.rem(h + dh, 2), z, c, qwrap(q + dq)))
    for dz in range(1, NZ):
        peers.append(dev(h, zwrap(z + dz), c, q))
    for peer in peers:
        pl.semaphore_signal(barrier, inc=1, device_id=peer, device_id_type=MESH)
    pl.semaphore_wait(barrier, len(peers))

    trade = rcopy(give_ref, xch, x_sem.at[0], x_sem.at[1], sib)
    trade.start()

    w_in = pltpu.make_async_copy(up_ref, wu.at[0], w_sem.at[0])
    w_in_give = rcopy(dn_ref, wd.at[0], w_sem.at[1], w_sem.at[2], sib)
    w_out = pltpu.make_async_copy(dn_ref, wd.at[1], w_sem.at[0])
    w_out_give = rcopy(up_ref, wu.at[1], w_sem.at[1], w_sem.at[2], sib)

    @pl.when(c == 0)
    def _():
        w_in.start()
        w_in_give.start()

    @pl.when(c == 1)
    def _():
        w_out.start()
        w_out_give.start()

    place0 = ids_ref[0:1, :] * CAP + slots_ref[0:1, :]
    place1 = ids_ref[1:2, :] * CAP + slots_ref[1:2, :]
    slot = lax.broadcasted_iota(jnp.int32, (ROWS, TOK), 0)
    hit0 = (slot == place0).astype(F32)
    hit1 = (slot == place1).astype(F32)
    pick[...] = (hit0 + hit1).astype(BF)
    lane8 = lax.broadcasted_iota(jnp.int32, (128, TOK), 0)
    expert = lax.rem(lane8, NE)
    live = lane8 < 3 * NE
    sign = jnp.where(live & (expert == ids_ref[0:1, :]), 1.0, 0.0) - jnp.where(
        live & (expert == ids_ref[1:2, :]), 1.0, 0.0
    )

    @pl.when(c == 0)
    def _():
        msend[...] = dot_nt((hit0 - hit1).astype(BF), sign.astype(BF)).astype(BF)

    ta_r[1, 1] = jnp.zeros((HALF, BLK), BF)
    tb_r[0, 1] = jnp.zeros((HALF, BLK), BF)
    tp_r[0, 1, pl.ds(QUART, QUART)] = jnp.zeros((QUART, BLK), BF)
    tp_r[1, 1, pl.ds(0, QUART)] = jnp.zeros((QUART, BLK), BF)
    pre[...] = jnp.zeros((ROWS, 2 * HID), F32)
    logit[...] = jnp.zeros((ROWS, 128), F32)

    trade.wait_recv()
    both = keep_ref[...] + xch[...]
    sent[...] = dot_nn(pick[...], both).astype(BF)

    mine = h * NZ + z

    def disp(dh, dq):
        qd = qwrap(q + dq)
        return rcopy(
            sent.at[rows_of(qd)], gath.at[mine, rows_of(q)], d_ssem.at[dh, dq], d_rsem.at[dh, dq],
            dev(lax.rem(h + dh, 2), z, c, qd),
        )

    def disp_land(dh, dq):
        land = gath.at[lax.rem(h + dh, 2) * NZ + z, rows_of(qwrap(q - dq))]
        return rcopy(land, land, d_ssem.at[dh, dq], d_rsem.at[dh, dq], sib)

    def meta_copy(dq):
        qd = qwrap(q + dq)
        return rcopy(
            msend.at[rows_of(qd)], meta.at[rows_of(q)], m_ssem.at[dq], m_rsem.at[dq], dev(h, z, c, qd)
        )

    def meta_land(dq):
        land = meta.at[rows_of(qwrap(q - dq))]
        return rcopy(land, land, m_ssem.at[dq], m_rsem.at[dq], sib)

    @pl.when(q < NE // 2)
    def _():
        for dq in range(NE):
            disp(1, dq).start()

    for dq in range(1, NE):
        disp(0, dq).start()

    @pl.when(c == 0)
    def _():
        for dq in range(1, NE):
            meta_copy(dq).start()
        meta[rows_of(q), :] = msend[rows_of(q), :]

    gath[mine, rows_of(q), :] = sent[rows_of(q), :]

    def zblock(hh, d, k):
        return hh * NZ + zwrap(z - k + 2 * d * k)

    def copy_a(d, k):
        ref = gath.at[zblock(h, d, k - 1), LO]
        return rcopy(ref, ref, a_ssem.at[d, k], a_rsem.at[d, k], znext(d))

    def land_a(d, k):
        ref = gath.at[zblock(h, d, k), LO]
        return rcopy(ref, ref, a_ssem.at[d, k], a_rsem.at[d, k], znext(d))

    def copy_b(d, k):
        ref = gath.at[zblock(h, d, k - 1), HI]
        return rcopy(ref, ref, b_ssem.at[d, k], b_rsem.at[d, k], znext(d))

    def land_b(d, k):
        ref = gath.at[zblock(h, d, k), HI]
        return rcopy(ref, ref, b_ssem.at[d, k], b_rsem.at[d, k], znext(d))

    def part_p(d, far):
        return pl.ds(d * QUART, QUART) if far else LO

    def copy_p(d, k, far):
        ref = gath.at[zblock(1 - h, d, k - 1), part_p(d, far)]
        return rcopy(ref, ref, p_ssem.at[d, k], p_rsem.at[d, k], znext(d))

    def land_p(d, k, far):
        ref = gath.at[zblock(1 - h, d, k), part_p(d, far)]
        return rcopy(ref, ref, p_ssem.at[d, k], p_rsem.at[d, k], znext(d))

    def copy_f(d, k):
        ref = gath.at[zblock(h, d, k), HI]
        return rcopy(ref, ref, f_ssem.at[d, k], f_rsem.at[d, k], partner)

    def land_f(d, k):
        ref = gath.at[zblock(1 - h, d, k), HI]
        return rcopy(ref, ref, f_ssem.at[d, k], f_rsem.at[d, k], partner)

    for dq in range(1, NE):
        disp_land(0, dq).wait_recv()
    for d in range(2):
        copy_a(d, 1).start()
        copy_b(d, 1).start()
    copy_f(0, 0).start()
    for dq in range(NE):

        @pl.when(qwrap(q - dq) < NE // 2)
        def _():
            disp_land(1, dq).wait_recv()

    for d in range(2):
        copy_p(d, 1, False).start()

    @pl.when(c == 0)
    def _():
        def split(p, carry):
            r = rt_ref[:, lanes(p)]
            top = r.astype(BF).astype(F32)
            mid = (r - top).astype(BF).astype(F32)
            low = r - top - mid
            rt3[:, lanes(p)] = jnp.concatenate([top, mid, low, jnp.zeros((104, BLK), F32)], axis=0).astype(BF)
            return carry

        lax.fori_loop(0, NBLK, split, 0)
        w_in.wait()
        w_out_give.wait_recv()
        for dq in range(1, NE):
            meta_land(dq).wait_recv()

    @pl.when(c == 1)
    def _():
        w_out.wait()
        w_in_give.wait_recv()

    def accumulate(p):
        @pl.when(c == 0)
        def _():
            x = gath[p]
            pre[:, 0:HID] += dot_nn(x, wu[0, lanes(p), :])
            pre[:, HID : 2 * HID] += dot_nn(x, wu[1, lanes(p), :])
            logit[...] += dot_nt(x, rt3[:, lanes(p)])

        @pl.when(c == 1)
        def _():
            x = gath[p]
            pre[:, 0:HID] += dot_nt(x, wd[0, :, lanes(p)])
            pre[:, HID : 2 * HID] += dot_nt(x, wd[1, :, lanes(p)])

    def gather_step(k, carry):
        near = k < FAR

        @pl.when((k >= 1) & (k <= FAR))
        def _():
            land_a(0, k).wait_recv()

            @pl.when(near)
            def _():
                copy_a(0, k + 1).start()

            land_b(1, k).wait_recv()

            @pl.when(near)
            def _():
                copy_b(1, k + 1).start()

            copy_f(1, k).start()

            @pl.when(near)
            def _():
                land_a(1, k).wait_recv()

                @pl.when(k < FAR - 1)
                def _():
                    copy_a(1, k + 1).start()

                land_b(0, k).wait_recv()

                @pl.when(k < FAR - 1)
                def _():
                    copy_b(0, k + 1).start()

                copy_f(0, k).start()
                for d in range(2):
                    land_p(d, k, False).wait_recv()

                    @pl.when(k < FAR - 1)
                    def _():
                        copy_p(d, k + 1, False).start()

                    @pl.when(k == FAR - 1)
                    def _():
                        copy_p(d, k + 1, True).start()

            @pl.when(k == FAR)
            def _():
                for d in range(2):
                    land_p(d, k, True).wait_recv()

        def block_step(j, carry2):
            d = lax.rem(j, 2)
            other = j // 2
            dist = k - other
            ok = (dist >= 0) & (dist <= FAR)
            ok = ok & ((d == 0) | ((dist >= 1) & (dist < FAR)))

            @pl.when(ok)
            def _():
                @pl.when(other == 1)
                def _():
                    dx = jnp.where(dist == FAR, 1, d)
                    land_f(dx, dist).wait_recv()

                accumulate(zblock(lax.rem(h + other, 2), d, dist))

            return carry2

        lax.fori_loop(0, 4, block_step, 0)
        return carry

    lax.fori_loop(0, FAR + 2, gather_step, 0)

    middle = rcopy(ms, mr, mid_sem.at[0], mid_sem.at[1], sib)

    @pl.when(c == 1)
    def _():
        ms[...] = pre[...].astype(BF)

    def gates():
        gap = jnp.sum(logit[...] * meta[...].astype(F32), axis=1, keepdims=True)
        return jax.nn.sigmoid(gap), jax.nn.sigmoid(-gap)

    @pl.when(c == 0)
    def _():
        gate, _ = gates()
        v = pre[...]
        ms[...] = (gate * (v * jax.nn.sigmoid(v))).astype(BF)

    middle.start()
    middle.wait_recv()

    @pl.when(c == 0)
    def _():
        gate, gate_other = gates()
        v = pre[...]
        u = mr[...].astype(F32)
        sg = jax.nn.sigmoid(v)
        pg[...] = (gate * u * (sg * (1.0 + v * (1.0 - sg)))).astype(BF)
        t = jnp.sum(v * sg * u, axis=1, keepdims=True) * gate * gate_other
        ts = t * meta[...].astype(F32)
        top = ts.astype(BF).astype(F32)
        lane = lax.broadcasted_iota(jnp.int32, (ROWS, 128), 1)
        tsb[...] = ts.astype(BF)
        tlb[...] = jnp.where(lane < NE, top, jnp.where(lane < 2 * NE, ts - top, 0.0)).astype(BF)

    def product(p, r):
        @pl.when(c == 0)
        def _():
            acc = dot_nt(pg[r, 0:HID], wu[0, lanes(p), :])
            acc += dot_nt(pg[r, HID : 2 * HID], wu[1, lanes(p), :])
            part[...] = acc + dot_nn(tsb[r, :], rt3[:, lanes(p)])

        @pl.when(c == 1)
        def _():
            acc = dot_nn(mr[r, 0:HID], wd[0, :, lanes(p)])
            part[...] = acc + dot_nn(mr[r, HID : 2 * HID], wd[1, :, lanes(p)])

    def tblock(hh, d, dist):
        return hh * NZ + zwrap(z + dist - 2 * d * dist)

    def copy_ra(d, t):
        return rcopy(ta_s.at[d, t], ta_r.at[d, t], ra_ssem.at[d, t], ra_rsem.at[d, t], znext(d))

    def copy_rb(d, t):
        return rcopy(tb_s.at[d, t], tb_r.at[d, t], rb_ssem.at[d, t], rb_rsem.at[d, t], znext(d))

    def copy_rp(d, t, far):
        rr = part_p(d, far)
        return rcopy(tp_s.at[d, t, rr], tp_r.at[d, t, rr], rp_ssem.at[d, t], rp_rsem.at[d, t], znext(d))

    def copy_rx(d, dist):
        return rcopy(xs.at[d, dist], xr.at[d, dist], rx_ssem.at[d, dist], rx_rsem.at[d, dist], partner)

    def wait_rp(d, t):
        @pl.when(t == 1)
        def _():
            copy_rp(d, 1, True).wait_recv()

        @pl.when(t > 1)
        def _():
            copy_rp(d, t, False).wait_recv()

    plane = [(dh, dq) for dh in range(2) for dq in range(NE) if dh or dq]

    def plane_dev(dh, dq):
        return lax.rem(h + dh, 2), qwrap(q + dq)

    def copy_g1(i, dh, dq):
        hh, qq = plane_dev(dh, dq)
        return rcopy(gp.at[hh * NE + qq], g1.at[i], g1_ssem.at[i], g1_rsem.at[i], dev(hh, z, c, qq))

    def copy_g2(dz):
        return rcopy(g2s, g2.at[dz], g2_ssem.at[dz], g2_rsem.at[dz], dev(h, zwrap(z + dz), c, q))

    me_p = h * NE + q

    def copy_g3(i, dh, dq):
        hh, qq = plane_dev(dh, dq)
        return rcopy(g3s, g3.at[me_p], g3_ssem.at[i], g3_rsem.at[i], dev(hh, z, c, qq))

    def land_g3(i, dh, dq):
        hh, qq = lax.rem(h + dh, 2), qwrap(q - dq)
        return rcopy(g3s, g3.at[hh * NE + qq], g3_ssem.at[i], g3_rsem.at[i], sib)

    g4 = rcopy(g3, gr_ref, g4_sem.at[0], g4_sem.at[1], sib)

    def router_stage(step):
        @pl.when((c == 0) & (step == 0))
        def _():
            tl = tlb[...]

            def one(p, carry):
                full = dot_tn(tl, gath[p])
                gp[p] = full[0:NE] + full[NE : 2 * NE]
                return carry

            lax.fori_loop(0, NBLK, one, 0)
            for i, (dh, dq) in enumerate(plane):
                copy_g1(i, dh, dq).start()

        @pl.when((c == 0) & (step == 2))
        def _():
            total = gp[me_p]
            for i, (dh, dq) in enumerate(plane):
                copy_g1(i, dh, dq).wait_recv()
                total = total + g1[i]
            g2s[...] = total
            for dz in range(1, NZ):
                copy_g2(dz).start()

        @pl.when((c == 0) & (step == 3))
        def _():
            total = g2s[...]
            for dz in range(1, NZ):
                copy_g2(dz).wait_recv()
                total = total + g2[dz]
            g3s[...] = total
            g3[me_p] = total
            for i, (dh, dq) in enumerate(plane):
                copy_g3(i, dh, dq).start()

        @pl.when((c == 0) & (step == 4))
        def _():
            for i, (dh, dq) in enumerate(plane):
                land_g3(i, dh, dq).wait_recv()
            g4.start()

    gu_own = pltpu.make_async_copy(gu.at[0], gu_ref, gsem.at[0])
    gu_give = rcopy(gu.at[1], gu_ref, gsem.at[1], gsem.at[2], sib)
    gd_own = pltpu.make_async_copy(gd.at[1], gd_ref, gsem.at[0])
    gd_give = rcopy(gd.at[0], gd_ref, gsem.at[1], gsem.at[2], sib)

    def weight_grads(step):
        def one(i, carry):
            p = step * 4 + i

            @pl.when(c == 0)
            def _():
                full = dot_tn(gath[p], pg[...]).astype(BF)
                gu[0, lanes(p), :] = full[:, 0:HID]
                gu[1, lanes(p), :] = full[:, HID : 2 * HID]

            @pl.when(c == 1)
            def _():
                full = dot_tn(mr[...], gath[p]).astype(BF)
                gd[0, :, lanes(p)] = full[0:HID]
                gd[1, :, lanes(p)] = full[HID : 2 * HID]

            return carry

        @pl.when(step < 4)
        def _():
            lax.fori_loop(0, 4, one, 0)

        @pl.when((step == 3) & (c == 0))
        def _():
            gu_own.start()
            gu_give.start()

        @pl.when((step == 3) & (c == 1))
        def _():
            gd_own.start()
            gd_give.start()

    last = FAR + 1

    def scatter_step(step, carry):
        dist = last - step
        nxt = FAR - step

        def side(d, carry2):
            @pl.when(((step == 0) & (d == 1)) | ((step >= 1) & (step < FAR)) | ((step == FAR) & (d == 0)))
            def _():
                product(tblock(1 - h, d, nxt), HI)
                xs[d, nxt] = part[...].astype(BF)
                copy_rx(d, nxt).start()

            @pl.when((((step == 1) | (step == last)) & (d == 0)) | ((step > 1) & (step < last)))
            def _():
                product(tblock(h, d, dist), LO)

                @pl.when(step == 1)
                def _():
                    ta_s[0, 1] = part[...].astype(BF)
                    copy_ra(0, 1).start()

                @pl.when((step > 1) & (step < last))
                def _():
                    @pl.when((step > 2) | (d == 0))
                    def _():
                        copy_ra(d, step - 1).wait_recv()

                    ta_s[d, step] = (part[...] + ta_r[d, step - 1].astype(F32)).astype(BF)
                    copy_ra(d, step).start()

                @pl.when(step == last)
                def _():
                    copy_ra(0, FAR).wait_recv()
                    copy_ra(1, FAR).wait_recv()
                    fs0[LO, :] = (part[...] + ta_r[0, FAR].astype(F32) + ta_r[1, FAR].astype(F32)).astype(BF)

            @pl.when((((step == 1) | (step == last)) & (d == 0)) | ((step > 1) & (step < last)))
            def _():
                product(tblock(1 - h, d, dist), LO)

                @pl.when(step == 1)
                def _():
                    both_halves = part[...].astype(BF)
                    tp_s[0, 1, pl.ds(0, QUART)] = both_halves[0:QUART]
                    tp_s[1, 1, pl.ds(QUART, QUART)] = both_halves[QUART:HALF]
                    copy_rp(0, 1, True).start()
                    copy_rp(1, 1, True).start()

                @pl.when((step > 1) & (step < last))
                def _():
                    wait_rp(d, step - 1)
                    tp_s[d, step] = (part[...] + tp_r[d, step - 1].astype(F32)).astype(BF)
                    copy_rp(d, step, False).start()

                @pl.when(step == last)
                def _():
                    copy_rp(0, FAR, False).wait_recv()
                    copy_rp(1, FAR, False).wait_recv()
                    fs1[...] = (part[...] + tp_r[0, FAR].astype(F32) + tp_r[1, FAR].astype(F32)).astype(BF)

            @pl.when(((step == 1) & (d == 1)) | ((step == last) & (d == 0)) | ((step > 1) & (step < last)))
            def _():
                product(tblock(h, d, dist), HI)
                copy_rx(d, dist).wait_recv()
                summed = part[...] + xr[d, dist].astype(F32)

                @pl.when(step == 1)
                def _():
                    tb_s[1, 1] = summed.astype(BF)
                    copy_rb(1, 1).start()

                @pl.when((step > 1) & (step < last))
                def _():
                    @pl.when((step > 2) | (d == 1))
                    def _():
                        copy_rb(d, step - 1).wait_recv()

                    tb_s[d, step] = (summed + tb_r[d, step - 1].astype(F32)).astype(BF)
                    copy_rb(d, step).start()

                @pl.when(step == last)
                def _():
                    copy_rb(0, FAR).wait_recv()
                    copy_rb(1, FAR).wait_recv()
                    fs0[HI, :] = (summed + tb_r[0, FAR].astype(F32) + tb_r[1, FAR].astype(F32)).astype(BF)

            return carry2

        lax.fori_loop(0, 2, side, 0)
        router_stage(step)
        weight_grads(step)
        return carry

    lax.fori_loop(0, last + 1, scatter_step, 0)

    def ret_copy0(dq):
        qd = qwrap(q + dq)
        return rcopy(fs0.at[rows_of(qd)], ret0.at[rows_of(q)], r_ssem.at[dq], r_rsem.at[dq], dev(h, z, c, qd))

    def ret_land0(dq):
        land = ret0.at[rows_of(qwrap(q - dq))]
        return rcopy(land, land, r_ssem.at[dq], r_rsem.at[dq], sib)

    def ret_copy1(qd):
        return rcopy(fs1.at[rows_of(qd)], ret1.at[rows_of(q)], q_ssem.at[qd], q_rsem.at[q], dev(1 - h, z, c, qd))

    def ret_land1(i):
        land = ret1.at[rows_of(i)]
        return rcopy(land, land, q_ssem.at[0], q_rsem.at[i], sib)

    for qd in range(NE // 2):
        ret_copy1(qd).start()
    for dq in range(1, NE):
        ret_copy0(dq).start()
    ret0[rows_of(q), :] = fs0[rows_of(q), :]
    for dq in range(1, NE):
        ret_land0(dq).wait_recv()
    chosen = pick[...]
    got = dot_tn(chosen, ret0[...])

    @pl.when(q >= NE // 2)
    def _():
        outs[...] = got.astype(BF)

    @pl.when(q < NE // 2)
    def _():
        for i in range(NE):
            ret_land1(i).wait_recv()
        outs[...] = (got + dot_tn(chosen, ret1[...])).astype(BF)

    final = rcopy(outs, outr, o_sem.at[0], o_sem.at[1], sib)
    final.start()

    trade.wait_send()

    @pl.when(q < NE // 2)
    def _():
        for dq in range(NE):
            disp(1, dq).wait_send()

    for dq in range(1, NE):
        disp(0, dq).wait_send()
        ret_copy0(dq).wait_send()
    for qd in range(NE // 2):
        ret_copy1(qd).wait_send()

    def drain(k, carry):
        @pl.when(k >= 1)
        def _():
            copy_a(0, k).wait_send()
            copy_b(1, k).wait_send()

            @pl.when(k < FAR)
            def _():
                for d in range(2):
                    copy_p(d, k, False).wait_send()
                copy_a(1, k).wait_send()
                copy_b(0, k).wait_send()
                copy_f(0, k).wait_send()

            @pl.when(k == FAR)
            def _():
                for d in range(2):
                    copy_p(d, k, True).wait_send()

            copy_f(1, k).wait_send()
            copy_rx(1, k).wait_send()

            @pl.when(k < FAR)
            def _():
                copy_rx(0, k).wait_send()

            @pl.when(k == 1)
            def _():
                copy_ra(0, 1).wait_send()
                copy_rb(1, 1).wait_send()
                for d in range(2):
                    copy_rp(d, 1, True).wait_send()

            @pl.when(k > 1)
            def _():
                for d in range(2):
                    copy_ra(d, k).wait_send()
                    copy_rb(d, k).wait_send()
                    copy_rp(d, k, False).wait_send()

        @pl.when(k == 0)
        def _():
            copy_f(0, 0).wait_send()
            copy_rx(0, 0).wait_send()

        return carry

    lax.fori_loop(0, FAR + 1, drain, 0)
    middle.wait_send()

    @pl.when(c == 0)
    def _():
        w_in_give.wait_send()
        for dq in range(1, NE):
            meta_copy(dq).wait_send()
        for i, (dh, dq) in enumerate(plane):
            copy_g1(i, dh, dq).wait_send()
            copy_g3(i, dh, dq).wait_send()
        for dz in range(1, NZ):
            copy_g2(dz).wait_send()
        gr_ref[...] = g3[...]
        g4.wait_send()
        gu_own.wait()
        gu_give.wait_send()
        gd_give.wait_recv()

    @pl.when(c == 1)
    def _():
        w_out_give.wait_send()
        g4.wait_recv()
        gd_own.wait()
        gd_give.wait_send()
        gu_give.wait_recv()

    final.wait()

    @pl.when(c == 0)
    def _():
        og_ref[...] = outs[...]
        om_ref[...] = outr[...]

    @pl.when(c == 1)
    def _():
        og_ref[...] = outr[...]
        om_ref[...] = outs[...]


def vm(*shape, dtype=BF):
    return pltpu.VMEM(shape, dtype)


def dma(*shape):
    return pltpu.SemaphoreType.DMA(shape)


def shards(tokens, expert_ids, slot_ids, router, up_weight, down_weight, cotangent):
    core = lax.rem(lax.axis_index("section"), 2)
    first = core == 0
    keep = jnp.where(first, tokens, cotangent)
    give = jnp.where(first, cotangent, tokens)
    zero = jnp.zeros_like(tokens)

    def padded(v):
        return jnp.concatenate([jnp.where(first, v, zero), jnp.where(first, zero, v)], axis=1)

    vspec = pl.BlockSpec(memory_space=pltpu.VMEM)
    aspec = pl.BlockSpec(memory_space=pl.ANY)
    om, og, gu, gd, gr = pl.pallas_call(
        kernel,
        out_shape=(
            jax.ShapeDtypeStruct((TOK, BLK), BF),
            jax.ShapeDtypeStruct((TOK, BLK), BF),
            jax.ShapeDtypeStruct((WIDTH, HID), BF),
            jax.ShapeDtypeStruct((HID, WIDTH), BF),
            jax.ShapeDtypeStruct((NBLK, NE, BLK), F32),
        ),
        in_specs=[vspec, vspec, vspec, vspec, vspec, aspec, aspec],
        out_specs=(vspec, vspec, aspec, aspec, vspec),
        scratch_shapes=[
            vm(NBLK, ROWS, BLK), vm(2, WIDTH, HID), vm(2, HID, WIDTH), vm(2, WIDTH, HID), vm(2, HID, WIDTH),
            vm(128, WIDTH), vm(ROWS, TOK), vm(TOK, BLK), vm(ROWS, BLK), vm(ROWS, 128), vm(ROWS, 128),
            vm(ROWS, 2 * HID, dtype=F32), vm(ROWS, 128, dtype=F32), vm(ROWS, 2 * HID), vm(ROWS, 2 * HID),
            vm(ROWS, 2 * HID), vm(ROWS, 128), vm(ROWS, 128), vm(HALF, BLK, dtype=F32),
            vm(2, 5, HALF, BLK), vm(2, 5, HALF, BLK), vm(2, 5, HALF, BLK), vm(2, 5, HALF, BLK),
            vm(2, 5, HALF, BLK), vm(2, 5, HALF, BLK), vm(2, 5, HALF, BLK), vm(2, 5, HALF, BLK),
            vm(ROWS, BLK), vm(HALF, BLK), vm(ROWS, BLK), vm(ROWS, BLK), vm(TOK, BLK), vm(TOK, BLK),
            vm(NBLK, NE, BLK, dtype=F32), vm(15, NE, BLK, dtype=F32), vm(NE, BLK, dtype=F32),
            vm(NZ, NE, BLK, dtype=F32), vm(NE, BLK, dtype=F32), vm(NBLK, NE, BLK, dtype=F32),
            dma(3), dma(2), dma(2, NE), dma(2, NE), dma(NE), dma(NE),
            dma(2, 5), dma(2, 5), dma(2, 5), dma(2, 5), dma(2, 5), dma(2, 5), dma(2, 5), dma(2, 5),
            dma(2), dma(2, 5), dma(2, 5), dma(2, 5), dma(2, 5), dma(2, 5), dma(2, 5), dma(2, 5), dma(2, 5),
            dma(3), dma(NE), dma(NE), dma(NE), dma(NE), dma(2),
            dma(15), dma(15), dma(NZ), dma(NZ), dma(15), dma(15), dma(2),
        ],
        compiler_params=pltpu.CompilerParams(
            collective_id=0, has_side_effects=True, vmem_limit_bytes=60 << 20
        ),
    )(
        padded(keep), padded(give), expert_ids.T, slot_ids.T, router.T, up_weight[0], down_weight[0]
    )
    mixed = jnp.where(first, om[:, :FEAT], om[:, FEAT:])
    grad_tokens = jnp.where(first, og[:, :FEAT], og[:, FEAT:])
    grad_router = gr.transpose(0, 2, 1).reshape(WIDTH, NE)
    return (mixed, grad_tokens, gu[None], gd[None], grad_router)


def solution(mesh):
    in_specs = (
        P("expert", "section"),
        P("expert", None),
        P("expert", None),
        P(),
        P("expert", None, "section"),
        P("expert", "section", None),
        P("expert", "section"),
    )
    out_specs = (
        P("expert", "section"),
        P("expert", "section"),
        P("expert", None, "section"),
        P("expert", "section", None),
        P(),
    )
    return jax.shard_map(shards, mesh=mesh, in_specs=in_specs, out_specs=out_specs, check_vma=False)
```

```python
import jax
import jax.numpy as jnp
from jax import lax
from jax.experimental import pallas as pl
from jax.experimental.pallas import tpu as pltpu
from jax.sharding import PartitionSpec as P

MESH = pl.DeviceIdType.MESH
NZ = 8
FAR = NZ // 2
NE = 8
CAP = 48
TOK = 192
FEAT = 192
BLK = 2 * FEAT
ROWS = NE * CAP
HALF = ROWS // 2
QUART = HALF // 2
HID = 256
WIDTH = 6144
NBLK = WIDTH // BLK
BF = jnp.bfloat16
F32 = jnp.float32
LO = pl.ds(0, HALF)
HI = pl.ds(HALF, HALF)


def dot_nn(a, b):
    return jnp.dot(a, b, preferred_element_type=F32)


def dot_nt(a, b):
    return lax.dot_general(a, b, (((1,), (1,)), ((), ())), preferred_element_type=F32)


def dot_tn(a, b):
    return lax.dot_general(a, b, (((0,), (0,)), ((), ())), preferred_element_type=F32)


def lanes(p):
    return pl.ds(pl.multiple_of(p * BLK, BLK), BLK)


def rows_of(q):
    return pl.ds(pl.multiple_of(q * CAP, CAP), CAP)


def kernel(
    tok_ref, cot_ref, ids_hbm, slots_hbm, rt_hbm, up_ref, dn_ref,
    om_ref, og_ref, gu_ref, gd_ref, gr_ref,
    gath, wu, wd, gu, gd, rt3, pick, keep, give, ids_ref, slots_ref, rt_ref, xch, sent, msend, meta,
    pre, logit, ms, mr, pg, tsb, tlb, part,
    ta_s, ta_r, tb_s, tb_r, tp_s, tp_r, xs, xr,
    fs0, fs1, ret0, ret1, outs, outo, outr,
    gp, g1, g2s, g2, g3s, g3,
    in_sem, w_sem, x_sem, d_ssem, d_rsem, m_ssem, m_rsem,
    a_ssem, a_rsem, b_ssem, b_rsem, p_ssem, p_rsem, f_ssem, f_rsem,
    mid_sem, ra_ssem, ra_rsem, rb_ssem, rb_rsem, rp_ssem, rp_rsem, rx_ssem, rx_rsem,
    gsem, r_ssem, r_rsem, q_ssem, q_rsem, o_sem,
    g1_ssem, g1_rsem, g2_ssem, g2_rsem, g3_ssem, g3_rsem, g4_sem,
):
    s = lax.axis_index("section")
    q = lax.axis_index("expert")
    c = lax.rem(s, 2)
    z = lax.rem(s // 2, NZ)
    h = s // (2 * NZ)

    def dev(hh, zz, cc, qq):
        return ((hh * NZ + zz) * 2 + cc, qq)

    def zwrap(v):
        return lax.rem(v + 2 * NZ, NZ)

    def qwrap(v):
        return lax.rem(v + NE, NE)

    sib = dev(h, z, 1 - c, q)
    partner = dev(1 - h, z, c, q)
    zdev = (dev(h, zwrap(z + 1), c, q), dev(h, zwrap(z - 1), c, q))

    def znext(d):
        return dev(h, zwrap(z + 1 - 2 * d), c, q)

    def rcopy(src, dst, ssem, rsem, target):
        return pltpu.make_async_remote_copy(
            src_ref=src, dst_ref=dst, send_sem=ssem, recv_sem=rsem, device_id=target, device_id_type=MESH
        )

    barrier = pltpu.get_barrier_semaphore()
    peers = [sib]
    for dh in range(2):
        for dq in range(NE):
            if dh or dq:
                peers.append(dev(lax.rem(h + dh, 2), z, c, qwrap(q + dq)))
    for dz in range(1, NZ):
        peers.append(dev(h, zwrap(z + dz), c, q))
    for peer in peers:
        pl.semaphore_signal(barrier, inc=1, device_id=peer, device_id_type=MESH)

    small = [
        pltpu.make_async_copy(ids_hbm, ids_ref, in_sem.at[0]),
        pltpu.make_async_copy(slots_hbm, slots_ref, in_sem.at[1]),
        pltpu.make_async_copy(rt_hbm, rt_ref, in_sem.at[2]),
    ]
    for copy in small:
        copy.start()
    tok_keep = pltpu.make_async_copy(tok_ref, keep, in_sem.at[3])
    cot_give = pltpu.make_async_copy(cot_ref, give, in_sem.at[4])
    cot_keep = pltpu.make_async_copy(cot_ref, keep, in_sem.at[3])
    tok_give = pltpu.make_async_copy(tok_ref, give, in_sem.at[4])
    w_in = pltpu.make_async_copy(up_ref, wu.at[0], w_sem.at[0])
    w_in_give = rcopy(dn_ref, wd.at[0], w_sem.at[1], w_sem.at[2], sib)
    w_out = pltpu.make_async_copy(dn_ref, wd.at[1], w_sem.at[0])
    w_out_give = rcopy(up_ref, wu.at[1], w_sem.at[1], w_sem.at[2], sib)

    @pl.when(c == 0)
    def _():
        cot_give.start()
        tok_keep.start()
        w_in.start()

    @pl.when(c == 1)
    def _():
        tok_give.start()
        cot_keep.start()
        w_out.start()

    small[0].wait()
    small[1].wait()

    place0 = ids_ref[0:1, :] * CAP + slots_ref[0:1, :]
    place1 = ids_ref[1:2, :] * CAP + slots_ref[1:2, :]
    slot = lax.broadcasted_iota(jnp.int32, (ROWS, TOK), 0)
    hit0 = (slot == place0).astype(F32)
    hit1 = (slot == place1).astype(F32)
    pick[...] = (hit0 + hit1).astype(BF)
    lane8 = lax.broadcasted_iota(jnp.int32, (128, TOK), 0)
    expert = lax.rem(lane8, NE)
    live = lane8 < 3 * NE
    sign = jnp.where(live & (expert == ids_ref[0:1, :]), 1.0, 0.0) - jnp.where(
        live & (expert == ids_ref[1:2, :]), 1.0, 0.0
    )

    @pl.when(c == 0)
    def _():
        msend[...] = dot_nt((hit0 - hit1).astype(BF), sign.astype(BF)).astype(BF)

    ta_r[1, 1] = jnp.zeros((HALF, BLK), BF)
    tb_r[0, 1] = jnp.zeros((HALF, BLK), BF)
    tp_r[0, 1, pl.ds(QUART, QUART)] = jnp.zeros((QUART, BLK), BF)
    tp_r[1, 1, pl.ds(0, QUART)] = jnp.zeros((QUART, BLK), BF)
    pre[...] = jnp.zeros((ROWS, 2 * HID), F32)
    logit[...] = jnp.zeros((ROWS, 128), F32)

    row = lax.broadcasted_iota(jnp.int32, (FEAT, BLK), 0)
    col = lax.broadcasted_iota(jnp.int32, (FEAT, BLK), 1)
    place_mine = (col == row + FEAT * c).astype(F32).astype(BF)
    place_other = (col == row + FEAT * (1 - c)).astype(F32).astype(BF)

    @pl.when(c == 0)
    def _():
        cot_give.wait()
        tok_keep.wait()

    @pl.when(c == 1)
    def _():
        tok_give.wait()
        cot_keep.wait()

    pl.semaphore_wait(barrier, len(peers))
    trade = rcopy(give, xch, x_sem.at[0], x_sem.at[1], sib)
    trade.start()
    half_both = dot_nn(keep[...], place_mine)
    trade.wait_recv()
    both = (half_both + dot_nn(xch[...], place_other)).astype(BF)
    sent[...] = dot_nn(pick[...], both).astype(BF)

    mine = h * NZ + z

    def disp(dh, dq):
        qd = qwrap(q + dq)
        return rcopy(
            sent.at[rows_of(qd)], gath.at[mine, rows_of(q)], d_ssem.at[dh, dq], d_rsem.at[dh, dq],
            dev(lax.rem(h + dh, 2), z, c, qd),
        )

    def disp_land(dh, dq):
        land = gath.at[lax.rem(h + dh, 2) * NZ + z, rows_of(qwrap(q - dq))]
        return rcopy(land, land, d_ssem.at[dh, dq], d_rsem.at[dh, dq], sib)

    def meta_copy(dq):
        qd = qwrap(q + dq)
        return rcopy(
            msend.at[rows_of(qd)], meta.at[rows_of(q)], m_ssem.at[dq], m_rsem.at[dq], dev(h, z, c, qd)
        )

    def meta_land(dq):
        land = meta.at[rows_of(qwrap(q - dq))]
        return rcopy(land, land, m_ssem.at[dq], m_rsem.at[dq], sib)

    for dq in range(1, NE):
        disp(0, dq).start()

    @pl.when(q < NE // 2)
    def _():
        for dq in range(NE):
            disp(1, dq).start()

    gath[mine, rows_of(q), :] = sent[rows_of(q), :]

    @pl.when(c == 0)
    def _():
        w_in_give.start()
        for dq in range(1, NE):
            meta_copy(dq).start()
        meta[rows_of(q), :] = msend[rows_of(q), :]

    @pl.when(c == 1)
    def _():
        w_out_give.start()

    small[2].wait()

    def zblock(hh, d, k):
        return hh * NZ + zwrap(z - k + 2 * d * k)

    def copy_a(d, k):
        ref = gath.at[zblock(h, d, k - 1), LO]
        return rcopy(ref, ref, a_ssem.at[d, k], a_rsem.at[d, k], znext(d))

    def land_a(d, k):
        ref = gath.at[zblock(h, d, k), LO]
        return rcopy(ref, ref, a_ssem.at[d, k], a_rsem.at[d, k], znext(d))

    def copy_b(d, k):
        ref = gath.at[zblock(h, d, k - 1), HI]
        return rcopy(ref, ref, b_ssem.at[d, k], b_rsem.at[d, k], znext(d))

    def land_b(d, k):
        ref = gath.at[zblock(h, d, k), HI]
        return rcopy(ref, ref, b_ssem.at[d, k], b_rsem.at[d, k], znext(d))

    def part_p(d, far):
        return pl.ds(d * QUART, QUART) if far else LO

    def copy_p(d, k, far):
        ref = gath.at[zblock(1 - h, d, k - 1), part_p(d, far)]
        return rcopy(ref, ref, p_ssem.at[d, k], p_rsem.at[d, k], znext(d))

    def land_p(d, k, far):
        ref = gath.at[zblock(1 - h, d, k), part_p(d, far)]
        return rcopy(ref, ref, p_ssem.at[d, k], p_rsem.at[d, k], znext(d))

    def copy_f(d, k):
        ref = gath.at[zblock(h, d, k), HI]
        return rcopy(ref, ref, f_ssem.at[d, k], f_rsem.at[d, k], partner)

    def land_f(d, k):
        ref = gath.at[zblock(1 - h, d, k), HI]
        return rcopy(ref, ref, f_ssem.at[d, k], f_rsem.at[d, k], partner)

    for dq in range(1, NE):
        disp_land(0, dq).wait_recv()
    for d in range(2):
        copy_a(d, 1).start()
        copy_b(d, 1).start()
    copy_f(0, 0).start()
    for dq in range(NE):

        @pl.when(qwrap(q - dq) < NE // 2)
        def _():
            disp_land(1, dq).wait_recv()

    for d in range(2):
        copy_p(d, 1, False).start()

    @pl.when(c == 0)
    def _():
        def split(p, carry):
            r = rt_ref[:, lanes(p)]
            top = r.astype(BF).astype(F32)
            mid = (r - top).astype(BF).astype(F32)
            low = r - top - mid
            rt3[:, lanes(p)] = jnp.concatenate([top, mid, low, jnp.zeros((104, BLK), F32)], axis=0).astype(BF)
            return carry

        lax.fori_loop(0, NBLK, split, 0)
        w_in.wait()
        w_out_give.wait_recv()
        for dq in range(1, NE):
            meta_land(dq).wait_recv()

    @pl.when(c == 1)
    def _():
        w_out.wait()
        w_in_give.wait_recv()

    def accumulate(p):
        @pl.when(c == 0)
        def _():
            x = gath[p]
            pre[:, 0:HID] += dot_nn(x, wu[0, lanes(p), :])
            pre[:, HID : 2 * HID] += dot_nn(x, wu[1, lanes(p), :])
            logit[...] += dot_nt(x, rt3[:, lanes(p)])

        @pl.when(c == 1)
        def _():
            x = gath[p]
            pre[:, 0:HID] += dot_nt(x, wd[0, :, lanes(p)])
            pre[:, HID : 2 * HID] += dot_nt(x, wd[1, :, lanes(p)])

    def gather_step(k, carry):
        near = k < FAR

        @pl.when((k >= 1) & (k <= FAR))
        def _():
            land_a(0, k).wait_recv()

            @pl.when(near)
            def _():
                copy_a(0, k + 1).start()

            land_b(1, k).wait_recv()

            @pl.when(near)
            def _():
                copy_b(1, k + 1).start()

            copy_f(1, k).start()

            @pl.when(near)
            def _():
                land_a(1, k).wait_recv()

                @pl.when(k < FAR - 1)
                def _():
                    copy_a(1, k + 1).start()

                land_b(0, k).wait_recv()

                @pl.when(k < FAR - 1)
                def _():
                    copy_b(0, k + 1).start()

                copy_f(0, k).start()
                for d in range(2):
                    land_p(d, k, False).wait_recv()

                    @pl.when(k < FAR - 1)
                    def _():
                        copy_p(d, k + 1, False).start()

                    @pl.when(k == FAR - 1)
                    def _():
                        copy_p(d, k + 1, True).start()

            @pl.when(k == FAR)
            def _():
                for d in range(2):
                    land_p(d, k, True).wait_recv()

        def block_step(j, carry2):
            d = lax.rem(j, 2)
            other = j // 2
            dist = k - other
            ok = (dist >= 0) & (dist <= FAR)
            ok = ok & ((d == 0) | ((dist >= 1) & (dist < FAR)))

            @pl.when(ok)
            def _():
                @pl.when(other == 1)
                def _():
                    dx = jnp.where(dist == FAR, 1, d)
                    land_f(dx, dist).wait_recv()

                accumulate(zblock(lax.rem(h + other, 2), d, dist))

            return carry2

        lax.fori_loop(0, 4, block_step, 0)
        return carry

    lax.fori_loop(0, FAR + 2, gather_step, 0)

    middle = rcopy(ms, mr, mid_sem.at[0], mid_sem.at[1], sib)

    @pl.when(c == 1)
    def _():
        ms[...] = pre[...].astype(BF)

    def gates():
        gap = jnp.sum(logit[...] * meta[...].astype(F32), axis=1, keepdims=True)
        return jax.nn.sigmoid(gap), jax.nn.sigmoid(-gap)

    @pl.when(c == 0)
    def _():
        gate, _ = gates()
        v = pre[...]
        ms[...] = (gate * (v * jax.nn.sigmoid(v))).astype(BF)

    middle.start()
    middle.wait_recv()

    @pl.when(c == 0)
    def _():
        gate, gate_other = gates()
        v = pre[...]
        u = mr[...].astype(F32)
        sg = jax.nn.sigmoid(v)
        pg[...] = (gate * u * (sg * (1.0 + v * (1.0 - sg)))).astype(BF)
        t = jnp.sum(v * sg * u, axis=1, keepdims=True) * gate * gate_other
        ts = t * meta[...].astype(F32)
        top = ts.astype(BF).astype(F32)
        lane = lax.broadcasted_iota(jnp.int32, (ROWS, 128), 1)
        tsb[...] = ts.astype(BF)
        tlb[...] = jnp.where(lane < NE, top, jnp.where(lane < 2 * NE, ts - top, 0.0)).astype(BF)

    def product(p, r):
        @pl.when(c == 0)
        def _():
            acc = dot_nt(pg[r, 0:HID], wu[0, lanes(p), :])
            acc += dot_nt(pg[r, HID : 2 * HID], wu[1, lanes(p), :])
            part[...] = acc + dot_nn(tsb[r, :], rt3[:, lanes(p)])

        @pl.when(c == 1)
        def _():
            acc = dot_nn(mr[r, 0:HID], wd[0, :, lanes(p)])
            part[...] = acc + dot_nn(mr[r, HID : 2 * HID], wd[1, :, lanes(p)])

    def tblock(hh, d, dist):
        return hh * NZ + zwrap(z + dist - 2 * d * dist)

    def copy_ra(d, t):
        return rcopy(ta_s.at[d, t], ta_r.at[d, t], ra_ssem.at[d, t], ra_rsem.at[d, t], znext(d))

    def copy_rb(d, t):
        return rcopy(tb_s.at[d, t], tb_r.at[d, t], rb_ssem.at[d, t], rb_rsem.at[d, t], znext(d))

    def copy_rp(d, t, far):
        rr = part_p(d, far)
        return rcopy(tp_s.at[d, t, rr], tp_r.at[d, t, rr], rp_ssem.at[d, t], rp_rsem.at[d, t], znext(d))

    def copy_rx(d, dist):
        return rcopy(xs.at[d, dist], xr.at[d, dist], rx_ssem.at[d, dist], rx_rsem.at[d, dist], partner)

    def wait_rp(d, t):
        @pl.when(t == 1)
        def _():
            copy_rp(d, 1, True).wait_recv()

        @pl.when(t > 1)
        def _():
            copy_rp(d, t, False).wait_recv()

    plane = [(dh, dq) for dh in range(2) for dq in range(NE) if dh or dq]

    def plane_dev(dh, dq):
        return lax.rem(h + dh, 2), qwrap(q + dq)

    def copy_g1(i, dh, dq):
        hh, qq = plane_dev(dh, dq)
        return rcopy(gp.at[hh * NE + qq], g1.at[i], g1_ssem.at[i], g1_rsem.at[i], dev(hh, z, c, qq))

    def copy_g2(dz):
        return rcopy(g2s, g2.at[dz], g2_ssem.at[dz], g2_rsem.at[dz], dev(h, zwrap(z + dz), c, q))

    me_p = h * NE + q

    def copy_g3(i, dh, dq):
        hh, qq = plane_dev(dh, dq)
        return rcopy(g3s, g3.at[me_p], g3_ssem.at[i], g3_rsem.at[i], dev(hh, z, c, qq))

    def land_g3(i, dh, dq):
        hh, qq = lax.rem(h + dh, 2), qwrap(q - dq)
        return rcopy(g3s, g3.at[hh * NE + qq], g3_ssem.at[i], g3_rsem.at[i], sib)

    g4 = rcopy(g3, g3, g4_sem.at[0], g4_sem.at[1], sib)

    def router_stage(step):
        @pl.when((c == 0) & (step == 0))
        def _():
            tl = tlb[...]

            def one(p, carry):
                full = dot_tn(tl, gath[p])
                gp[p] = full[0:NE] + full[NE : 2 * NE]
                return carry

            lax.fori_loop(0, NBLK, one, 0)
            for i, (dh, dq) in enumerate(plane):
                copy_g1(i, dh, dq).start()

        @pl.when((c == 0) & (step == 2))
        def _():
            total = gp[me_p]
            for i, (dh, dq) in enumerate(plane):
                copy_g1(i, dh, dq).wait_recv()
                total = total + g1[i]
            g2s[...] = total
            for dz in range(1, NZ):
                copy_g2(dz).start()

        @pl.when((c == 0) & (step == 3))
        def _():
            total = g2s[...]
            for dz in range(1, NZ):
                copy_g2(dz).wait_recv()
                total = total + g2[dz]
            g3s[...] = total
            g3[me_p] = total
            for i, (dh, dq) in enumerate(plane):
                copy_g3(i, dh, dq).start()

        @pl.when((c == 0) & (step == 4))
        def _():
            for i, (dh, dq) in enumerate(plane):
                land_g3(i, dh, dq).wait_recv()
            g4.start()

    gu_give = rcopy(gu, gu_ref, gsem.at[1], gsem.at[2], sib)
    gd_give = rcopy(gd, gd_ref, gsem.at[1], gsem.at[2], sib)

    def weight_grads(step):
        def one(i, carry):
            p = step * 4 + i

            @pl.when(c == 0)
            def _():
                full = dot_tn(gath[p], pg[...]).astype(BF)
                gu_ref[lanes(p), :] = full[:, 0:HID]
                gu[lanes(p), :] = full[:, HID : 2 * HID]

            @pl.when(c == 1)
            def _():
                full = dot_tn(mr[...], gath[p]).astype(BF)
                gd[:, lanes(p)] = full[0:HID]
                gd_ref[:, lanes(p)] = full[HID : 2 * HID]

            return carry

        @pl.when(step < 4)
        def _():
            lax.fori_loop(0, 4, one, 0)

        @pl.when((step == 3) & (c == 0))
        def _():
            gu_give.start()

        @pl.when((step == 3) & (c == 1))
        def _():
            gd_give.start()

    def ret_copy0(dq):
        qd = qwrap(q + dq)
        return rcopy(fs0.at[rows_of(qd)], ret0.at[rows_of(q)], r_ssem.at[dq], r_rsem.at[dq], dev(h, z, c, qd))

    def ret_land0(dq):
        land = ret0.at[rows_of(qwrap(q - dq))]
        return rcopy(land, land, r_ssem.at[dq], r_rsem.at[dq], sib)

    def ret_copy1(qd):
        return rcopy(fs1.at[rows_of(qd)], ret1.at[rows_of(q)], q_ssem.at[qd], q_rsem.at[q], dev(1 - h, z, c, qd))

    def ret_land1(i):
        land = ret1.at[rows_of(i)]
        return rcopy(land, land, q_ssem.at[0], q_rsem.at[i], sib)

    last = FAR + 1

    def scatter_step(step, carry):
        dist = last - step
        nxt = FAR - step

        def share(d, carry2):
            @pl.when(((step == 0) & (d == 1)) | ((step >= 1) & (step < FAR)) | ((step == FAR) & (d == 0)))
            def _():
                product(tblock(1 - h, d, nxt), HI)
                xs[d, nxt] = part[...].astype(BF)
                copy_rx(d, nxt).start()

            return carry2

        lax.fori_loop(0, 2, share, 0)

        def own_first(d, carry2):
            @pl.when((((step == 1) | (step == last)) & (d == 0)) | ((step > 1) & (step < last)))
            def _():
                product(tblock(h, d, dist), LO)

                @pl.when(step == 1)
                def _():
                    ta_s[0, 1] = part[...].astype(BF)
                    copy_ra(0, 1).start()

                @pl.when((step > 1) & (step < last))
                def _():
                    @pl.when((step > 2) | (d == 0))
                    def _():
                        copy_ra(d, step - 1).wait_recv()

                    ta_s[d, step] = (part[...] + ta_r[d, step - 1].astype(F32)).astype(BF)
                    copy_ra(d, step).start()

                @pl.when(step == last)
                def _():
                    copy_ra(0, FAR).wait_recv()
                    copy_ra(1, FAR).wait_recv()
                    fs0[LO, :] = (part[...] + ta_r[0, FAR].astype(F32) + ta_r[1, FAR].astype(F32)).astype(BF)
                    for dq in range(NE):

                        @pl.when(qwrap(q + dq) < NE // 2)
                        def _():
                            if dq:
                                ret_copy0(dq).start()
                            else:
                                ret0[rows_of(q), :] = fs0[rows_of(q), :]

            return carry2

        lax.fori_loop(0, 2, own_first, 0)

        def other_first(d, carry2):
            @pl.when((((step == 1) | (step == last)) & (d == 0)) | ((step > 1) & (step < last)))
            def _():
                product(tblock(1 - h, d, dist), LO)

                @pl.when(step == 1)
                def _():
                    both_halves = part[...].astype(BF)
                    tp_s[0, 1, pl.ds(0, QUART)] = both_halves[0:QUART]
                    tp_s[1, 1, pl.ds(QUART, QUART)] = both_halves[QUART:HALF]
                    copy_rp(0, 1, True).start()
                    copy_rp(1, 1, True).start()

                @pl.when((step > 1) & (step < last))
                def _():
                    wait_rp(d, step - 1)
                    tp_s[d, step] = (part[...] + tp_r[d, step - 1].astype(F32)).astype(BF)
                    copy_rp(d, step, False).start()

                @pl.when(step == last)
                def _():
                    copy_rp(0, FAR, False).wait_recv()
                    copy_rp(1, FAR, False).wait_recv()
                    fs1[...] = (part[...] + tp_r[0, FAR].astype(F32) + tp_r[1, FAR].astype(F32)).astype(BF)
                    for qd in range(NE // 2):
                        ret_copy1(qd).start()

            return carry2

        lax.fori_loop(0, 2, other_first, 0)

        def own_second(d, carry2):
            @pl.when(((step == 1) & (d == 1)) | ((step == last) & (d == 0)) | ((step > 1) & (step < last)))
            def _():
                product(tblock(h, d, dist), HI)
                copy_rx(d, dist).wait_recv()
                summed = part[...] + xr[d, dist].astype(F32)

                @pl.when(step == 1)
                def _():
                    tb_s[1, 1] = summed.astype(BF)
                    copy_rb(1, 1).start()

                @pl.when((step > 1) & (step < last))
                def _():
                    @pl.when((step > 2) | (d == 1))
                    def _():
                        copy_rb(d, step - 1).wait_recv()

                    tb_s[d, step] = (summed + tb_r[d, step - 1].astype(F32)).astype(BF)
                    copy_rb(d, step).start()

                @pl.when(step == last)
                def _():
                    copy_rb(0, FAR).wait_recv()
                    copy_rb(1, FAR).wait_recv()
                    fs0[HI, :] = (summed + tb_r[0, FAR].astype(F32) + tb_r[1, FAR].astype(F32)).astype(BF)
                    for dq in range(NE):

                        @pl.when(qwrap(q + dq) >= NE // 2)
                        def _():
                            if dq:
                                ret_copy0(dq).start()
                            else:
                                ret0[rows_of(q), :] = fs0[rows_of(q), :]

            return carry2

        lax.fori_loop(0, 2, own_second, 0)
        router_stage(step)
        weight_grads(step)
        return carry

    lax.fori_loop(0, last + 1, scatter_step, 0)

    for dq in range(1, NE):
        ret_land0(dq).wait_recv()
    chosen = pick[...]
    got = dot_tn(chosen, ret0[...])

    def give_out(total):
        rounded = total.astype(BF)
        outo[...] = dot_nt(rounded, place_other).astype(BF)
        final.start()
        outs[...] = dot_nt(rounded, place_mine).astype(BF)

    final = rcopy(outo, outr, o_sem.at[0], o_sem.at[1], sib)

    @pl.when(q >= NE // 2)
    def _():
        give_out(got)

    @pl.when(q < NE // 2)
    def _():
        for i in range(NE):
            ret_land1(i).wait_recv()
        give_out(got + dot_tn(chosen, ret1[...]))

    trade.wait_send()

    @pl.when(q < NE // 2)
    def _():
        for dq in range(NE):
            disp(1, dq).wait_send()

    for dq in range(1, NE):
        disp(0, dq).wait_send()
        ret_copy0(dq).wait_send()
    for qd in range(NE // 2):
        ret_copy1(qd).wait_send()

    def drain(k, carry):
        @pl.when(k >= 1)
        def _():
            copy_a(0, k).wait_send()
            copy_b(1, k).wait_send()

            @pl.when(k < FAR)
            def _():
                for d in range(2):
                    copy_p(d, k, False).wait_send()
                copy_a(1, k).wait_send()
                copy_b(0, k).wait_send()
                copy_f(0, k).wait_send()

            @pl.when(k == FAR)
            def _():
                for d in range(2):
                    copy_p(d, k, True).wait_send()

            copy_f(1, k).wait_send()
            copy_rx(1, k).wait_send()

            @pl.when(k < FAR)
            def _():
                copy_rx(0, k).wait_send()

            @pl.when(k == 1)
            def _():
                copy_ra(0, 1).wait_send()
                copy_rb(1, 1).wait_send()
                for d in range(2):
                    copy_rp(d, 1, True).wait_send()

            @pl.when(k > 1)
            def _():
                for d in range(2):
                    copy_ra(d, k).wait_send()
                    copy_rb(d, k).wait_send()
                    copy_rp(d, k, False).wait_send()

        @pl.when(k == 0)
        def _():
            copy_f(0, 0).wait_send()
            copy_rx(0, 0).wait_send()

        return carry

    lax.fori_loop(0, FAR + 1, drain, 0)
    middle.wait_send()

    @pl.when(c == 0)
    def _():
        w_in_give.wait_send()
        for dq in range(1, NE):
            meta_copy(dq).wait_send()
        for i, (dh, dq) in enumerate(plane):
            copy_g1(i, dh, dq).wait_send()
            copy_g3(i, dh, dq).wait_send()
        for dz in range(1, NZ):
            copy_g2(dz).wait_send()
        g4.wait_send()
        gu_give.wait_send()
        gd_give.wait_recv()

    @pl.when(c == 1)
    def _():
        w_out_give.wait_send()
        g4.wait_recv()
        gd_give.wait_send()
        gu_give.wait_recv()

    for p in range(NBLK):
        gr_ref[:, p * BLK : (p + 1) * BLK] = g3[p]
    final.wait()

    @pl.when(c == 0)
    def _():
        og_ref[...] = outs[...]
        om_ref[...] = outr[...]

    @pl.when(c == 1)
    def _():
        og_ref[...] = outr[...]
        om_ref[...] = outs[...]


def vm(*shape, dtype=BF):
    return pltpu.VMEM(shape, dtype)


def dma(*shape):
    return pltpu.SemaphoreType.DMA(shape)


def store(om, og, gu, gd, gr, om_out, og_out, gu_out, gd_out, gr_out, sem):
    copies = [
        pltpu.make_async_copy(src, dst, sem.at[i])
        for i, (src, dst) in enumerate(((gu, gu_out), (gd, gd_out), (om, om_out), (og, og_out), (gr, gr_out)))
    ]
    for copy in copies:
        copy.start()
    for copy in copies:
        copy.wait()


def shards(tokens, expert_ids, slot_ids, router, up_weight, down_weight, cotangent):
    vspec = pl.BlockSpec(memory_space=pltpu.VMEM)
    aspec = pl.BlockSpec(memory_space=pl.ANY)
    hspec = pl.BlockSpec(memory_space=pltpu.HBM)
    shapes = (
        jax.ShapeDtypeStruct((TOK, FEAT), BF),
        jax.ShapeDtypeStruct((TOK, FEAT), BF),
        jax.ShapeDtypeStruct((WIDTH, HID), BF),
        jax.ShapeDtypeStruct((HID, WIDTH), BF),
        jax.ShapeDtypeStruct((NE, WIDTH), F32),
    )
    results = pl.pallas_call(
        kernel,
        out_shape=(
            *shapes,
        ),
        in_specs=[hspec] * 7,
        out_specs=(vspec,) * 5,
        scratch_shapes=[
            vm(NBLK, ROWS, BLK), vm(2, WIDTH, HID), vm(2, HID, WIDTH), vm(WIDTH, HID), vm(HID, WIDTH),
            vm(128, WIDTH), vm(ROWS, TOK), vm(TOK, FEAT), vm(TOK, FEAT),
            vm(2, TOK, dtype=jnp.int32), vm(2, TOK, dtype=jnp.int32), vm(NE, WIDTH, dtype=F32),
            vm(TOK, FEAT), vm(ROWS, BLK), vm(ROWS, 128), vm(ROWS, 128),
            vm(ROWS, 2 * HID, dtype=F32), vm(ROWS, 128, dtype=F32), vm(ROWS, 2 * HID), vm(ROWS, 2 * HID),
            vm(ROWS, 2 * HID), vm(ROWS, 128), vm(ROWS, 128), vm(HALF, BLK, dtype=F32),
            vm(2, 5, HALF, BLK), vm(2, 5, HALF, BLK), vm(2, 5, HALF, BLK), vm(2, 5, HALF, BLK),
            vm(2, 5, HALF, BLK), vm(2, 5, HALF, BLK), vm(2, 5, HALF, BLK), vm(2, 5, HALF, BLK),
            vm(ROWS, BLK), vm(HALF, BLK), vm(ROWS, BLK), vm(ROWS, BLK), vm(TOK, FEAT), vm(TOK, FEAT), vm(TOK, FEAT),
            vm(NBLK, NE, BLK, dtype=F32), vm(15, NE, BLK, dtype=F32), vm(NE, BLK, dtype=F32),
            vm(NZ, NE, BLK, dtype=F32), vm(NE, BLK, dtype=F32), vm(NBLK, NE, BLK, dtype=F32),
            dma(5), dma(3), dma(2), dma(2, NE), dma(2, NE), dma(NE), dma(NE),
            dma(2, 5), dma(2, 5), dma(2, 5), dma(2, 5), dma(2, 5), dma(2, 5), dma(2, 5), dma(2, 5),
            dma(2), dma(2, 5), dma(2, 5), dma(2, 5), dma(2, 5), dma(2, 5), dma(2, 5), dma(2, 5), dma(2, 5),
            dma(3), dma(NE), dma(NE), dma(NE), dma(NE), dma(2),
            dma(15), dma(15), dma(NZ), dma(NZ), dma(15), dma(15), dma(2),
        ],
        compiler_params=pltpu.CompilerParams(
            collective_id=0, has_side_effects=True, vmem_limit_bytes=44 << 20
        ),
    )(
        *(
            pltpu.with_memory_space_constraint(v, pltpu.HBM)
            for v in (tokens, cotangent, expert_ids.T, slot_ids.T, router.T, up_weight[0], down_weight[0])
        )
    )
    mixed, grad_tokens, gu, gd, gr = pl.pallas_call(
        store,
        out_shape=shapes,
        in_specs=[aspec] * 5,
        out_specs=(hspec,) * 5,
        scratch_shapes=[dma(5)],
        compiler_params=pltpu.CompilerParams(vmem_limit_bytes=1 << 20),
    )(*results)
    return (mixed, grad_tokens, gu[None], gd[None], gr.T)


def solution(mesh):
    in_specs = (
        P("expert", "section"),
        P("expert", None),
        P("expert", None),
        P(),
        P("expert", None, "section"),
        P("expert", "section", None),
        P("expert", "section"),
    )
    out_specs = (
        P("expert", "section"),
        P("expert", "section"),
        P("expert", None, "section"),
        P("expert", "section", None),
        P(),
    )
    return jax.shard_map(shards, mesh=mesh, in_specs=in_specs, out_specs=out_specs, check_vma=False)
```

```python
import jax
import jax.numpy as jnp
from jax import lax
from jax.experimental import pallas as pl
from jax.experimental.pallas import tpu as pltpu
from jax.sharding import PartitionSpec as P

MESH = pl.DeviceIdType.MESH
NZ = 8
FAR = NZ // 2
NE = 8
CAP = 48
TOK = 192
FEAT = 192
BLK = 2 * FEAT
ROWS = NE * CAP
HALF = ROWS // 2
QUART = HALF // 2
HID = 256
WIDTH = 6144
NBLK = WIDTH // BLK
BF = jnp.bfloat16
F32 = jnp.float32
NY = NE // 2


def dot_nn(a, b):
    return jnp.dot(a, b, preferred_element_type=F32)


def dot_nt(a, b):
    return lax.dot_general(a, b, (((1,), (1,)), ((), ())), preferred_element_type=F32)


def dot_tn(a, b):
    return lax.dot_general(a, b, (((0,), (0,)), ((), ())), preferred_element_type=F32)


def lanes(p):
    return pl.ds(pl.multiple_of(p * BLK, BLK), BLK)


def rows_of(q):
    return pl.ds(pl.multiple_of(q * CAP, CAP), CAP)


def kernel(
    tok_ref, cot_ref, ids_hbm, slots_hbm, rt_hbm, up_ref, dn_ref,
    om_ref, og_ref, gu_ref, gd_ref, gr_ref,
    gath, wu, wd, gu, gd, gu0, gd0, rt3, pick, keep, give, ids_ref, slots_ref, rt_ref, xch, sent, msend, meta,
    pre, logit, ms, mr, pg, tsb, tlb, part,
    ring_s, ring_r, xs, xr,
    fs0, fs1, ret0, ret1,
    gp, g1, g2s, g2, g3s, g3,
    in_sem, w_sem, x_sem, d_ssem, d_rsem, m_ssem, m_rsem,
    ag_ssem, ag_rsem, f_ssem, f_rsem, mid_sem, rs_ssem, rs_rsem, rx_ssem, rx_rsem,
    gsem, r_ssem, r_rsem, o_sem,
    g1_ssem, g1_rsem, g2_ssem, g2_rsem, g3_ssem, g3_rsem, g4_sem,
):
    s = lax.axis_index("section")
    q = lax.axis_index("expert")
    c = lax.rem(s, 2)
    z = lax.rem(s // 2, NZ)
    h = s // (2 * NZ)

    def dev(hh, zz, cc, qq):
        return ((hh * NZ + zz) * 2 + cc, qq)

    def zwrap(v):
        return lax.rem(v + 2 * NZ, NZ)

    def qwrap(v):
        return lax.rem(v + NE, NE)

    lo_x = q // NY
    y = lax.rem(q, NY)

    def first(off=0, size=HALF):
        return pl.ds(pl.multiple_of((1 - lo_x) * HALF + off, QUART), size)

    def second(off=0, size=HALF):
        return pl.ds(pl.multiple_of(lo_x * HALF + off, QUART), size)

    def group(same, dy):
        return (lo_x if same else 1 - lo_x) * NY + lax.rem(y + NY + dy, NY)

    sib = dev(h, z, 1 - c, q)
    partner = dev(1 - h, z, c, q)

    def znext(d):
        return dev(h, zwrap(z + 1 - 2 * d), c, q)

    def rcopy(src, dst, ssem, rsem, target):
        return pltpu.make_async_remote_copy(
            src_ref=src, dst_ref=dst, send_sem=ssem, recv_sem=rsem, device_id=target, device_id_type=MESH
        )

    barrier = pltpu.get_barrier_semaphore()
    peers = [sib]
    for dh in range(2):
        for dq in range(NE):
            if dh or dq:
                peers.append(dev(lax.rem(h + dh, 2), z, c, qwrap(q + dq)))
    for dz in range(1, NZ):
        peers.append(dev(h, zwrap(z + dz), c, q))
    for peer in peers:
        pl.semaphore_signal(barrier, inc=1, device_id=peer, device_id_type=MESH)

    small = [
        pltpu.make_async_copy(ids_hbm, ids_ref, in_sem.at[0]),
        pltpu.make_async_copy(slots_hbm, slots_ref, in_sem.at[1]),
        pltpu.make_async_copy(rt_hbm, rt_ref, in_sem.at[2]),
    ]
    for copy in small:
        copy.start()
    tok_keep = pltpu.make_async_copy(tok_ref, keep, in_sem.at[3])
    cot_give = pltpu.make_async_copy(cot_ref, give, in_sem.at[4])
    cot_keep = pltpu.make_async_copy(cot_ref, keep, in_sem.at[3])
    tok_give = pltpu.make_async_copy(tok_ref, give, in_sem.at[4])
    w_in = pltpu.make_async_copy(up_ref, wu.at[0], w_sem.at[0])
    w_in_give = rcopy(dn_ref, wd.at[0], w_sem.at[1], w_sem.at[2], sib)
    w_out = pltpu.make_async_copy(dn_ref, wd.at[1], w_sem.at[0])
    w_out_give = rcopy(up_ref, wu.at[1], w_sem.at[1], w_sem.at[2], sib)

    @pl.when(c == 0)
    def _():
        cot_give.start()
        tok_keep.start()
        w_in.start()

    @pl.when(c == 1)
    def _():
        tok_give.start()
        cot_keep.start()
        w_out.start()

    @pl.when(c == 0)
    def _():
        cot_give.wait()
        tok_keep.wait()

    @pl.when(c == 1)
    def _():
        tok_give.wait()
        cot_keep.wait()

    pl.semaphore_wait(barrier, len(peers))
    trade = rcopy(give, xch, x_sem.at[0], x_sem.at[1], sib)
    trade.start()
    row = lax.broadcasted_iota(jnp.int32, (FEAT, BLK), 0)
    col = lax.broadcasted_iota(jnp.int32, (FEAT, BLK), 1)
    place_mine = (col == row + FEAT * c).astype(F32).astype(BF)
    place_other = (col == row + FEAT * (1 - c)).astype(F32).astype(BF)

    small[0].wait()
    small[1].wait()

    place0 = ids_ref[0:1, :] * CAP + slots_ref[0:1, :]
    place1 = ids_ref[1:2, :] * CAP + slots_ref[1:2, :]
    slot = lax.broadcasted_iota(jnp.int32, (ROWS, TOK), 0)
    hit0 = (slot == place0).astype(F32)
    hit1 = (slot == place1).astype(F32)
    pick[...] = (hit0 + hit1).astype(BF)
    half_both = dot_nn(keep[...], place_mine)
    trade.wait_recv()
    both = (half_both + dot_nn(xch[...], place_other)).astype(BF)
    sent[...] = dot_nn(pick[...], both).astype(BF)

    mine = h * NZ + z

    def disp(kind, dy):
        qd = group(kind == 0, dy)
        return rcopy(
            sent.at[rows_of(qd)], gath.at[mine, rows_of(q)], d_ssem.at[kind], d_rsem.at[kind],
            dev(1 - h if kind == 2 else h, z, c, qd),
        )

    def rows_in(ref, kind):
        return ref.at[pl.ds(0, (NY - 1 if kind == 0 else NY) * CAP)]

    def disp_all(kind):
        ref = rows_in(sent, kind)
        return rcopy(ref, ref, d_ssem.at[kind], d_rsem.at[kind], sib)

    def meta_copy(dq):
        qd = qwrap(q + dq)
        return rcopy(
            msend.at[rows_of(qd)], meta.at[rows_of(q)], m_ssem.at[0], m_rsem.at[0], dev(h, z, c, qd)
        )

    meta_all = rcopy(
        msend.at[pl.ds(0, ROWS - CAP)], msend.at[pl.ds(0, ROWS - CAP)], m_ssem.at[0], m_rsem.at[0], sib
    )

    plane_kinds = [(0, dy) for dy in range(1, NY)] + [(kind, dy) for kind in (1, 2) for dy in range(NY)]
    for kind, dy in plane_kinds:
        disp(kind, dy).start()

    gath[mine, rows_of(q), :] = sent[rows_of(q), :]

    lane8 = lax.broadcasted_iota(jnp.int32, (128, TOK), 0)
    expert = lax.rem(lane8, NE)
    live = lane8 < 3 * NE
    sign = jnp.where(live & (expert == ids_ref[0:1, :]), 1.0, 0.0) - jnp.where(
        live & (expert == ids_ref[1:2, :]), 1.0, 0.0
    )

    @pl.when(c == 0)
    def _():
        w_in_give.start()
        again = lax.broadcasted_iota(jnp.int32, (ROWS, TOK), 0)
        p0 = ids_ref[0:1, :] * CAP + slots_ref[0:1, :]
        p1 = ids_ref[1:2, :] * CAP + slots_ref[1:2, :]
        which = (again == p0).astype(F32) - (again == p1).astype(F32)
        msend[...] = dot_nt(which.astype(BF), sign.astype(BF)).astype(BF)
        for dq in range(1, NE):
            meta_copy(dq).start()
        meta[rows_of(q), :] = msend[rows_of(q), :]

    @pl.when(c == 1)
    def _():
        w_out_give.start()

    pre[...] = jnp.zeros((ROWS, 2 * HID), F32)
    logit[...] = jnp.zeros((ROWS, 128), F32)

    small[2].wait()

    def zblock(hh, d, k):
        return hh * NZ + zwrap(z - k + 2 * d * k)

    def piece(st, d, far):
        rows = second if st == 0 else first
        return rows(d * QUART, QUART) if far else rows()

    def ring(st, d, k, far, back):
        ref = gath.at[zblock(1 - h if st == 2 else h, d, k - back), piece(st, d, far)]
        return rcopy(ref, ref, ag_ssem.at[st, d], ag_rsem.at[st, d, k - 1], znext(d))

    def copy_f(d, k):
        ref = gath.at[zblock(h, d, k), second()]
        return rcopy(ref, ref, f_ssem.at[d], f_rsem.at[d, k], partner)

    def land_f(d, k):
        ref = gath.at[zblock(1 - h, d, k), second()]
        return rcopy(ref, ref, f_ssem.at[d], f_rsem.at[d, k], partner)

    disp_all(0).wait_recv()
    for d in range(2):
        ring(0, d, 1, False, 1).start()
    copy_f(0, 0).start()
    for st in (1, 2):
        disp_all(st).wait_recv()
        for d in range(2):
            ring(st, d, 1, False, 1).start()

    @pl.when(c == 0)
    def _():
        def split(p, carry):
            r = rt_ref[:, lanes(p)]
            top = r.astype(BF).astype(F32)
            mid = (r - top).astype(BF).astype(F32)
            low = r - top - mid
            rt3[:, lanes(p)] = jnp.concatenate([top, mid, low, jnp.zeros((104, BLK), F32)], axis=0).astype(BF)
            return carry

        lax.fori_loop(0, NBLK, split, 0)
        w_in.wait()
        w_out_give.wait_recv()
        meta_all.wait_recv()

    @pl.when(c == 1)
    def _():
        w_out.wait()
        w_in_give.wait_recv()

    def accumulate(p):
        @pl.when(c == 0)
        def _():
            x = gath[p]
            pre[:, 0:HID] += dot_nn(x, wu[0, lanes(p), :])
            pre[:, HID : 2 * HID] += dot_nn(x, wu[1, lanes(p), :])
            logit[...] += dot_nt(x, rt3[:, lanes(p)])

        @pl.when(c == 1)
        def _():
            x = gath[p]
            pre[:, 0:HID] += dot_nt(x, wd[0, :, lanes(p)])
            pre[:, HID : 2 * HID] += dot_nt(x, wd[1, :, lanes(p)])

    def gather_step(k, carry):
        @pl.when((k >= 1) & (k < FAR))
        def _():
            for st in range(3):
                for d in range(2):
                    ring(st, d, k, False, 0).wait_recv()
                    ring(st, d, k, False, 1).wait_send()

                    @pl.when(k < FAR - 1)
                    def _():
                        ring(st, d, k + 1, False, 1).start()

                    @pl.when(k == FAR - 1)
                    def _():
                        ring(st, d, k + 1, True, 1).start()

                    if st == 0:
                        if d == 0:
                            copy_f(0, k - 1).wait_send()
                        else:

                            @pl.when(k > 1)
                            def _():
                                copy_f(1, k - 1).wait_send()

                        copy_f(d, k).start()

        @pl.when(k == FAR)
        def _():
            for st in range(3):
                for d in range(2):
                    ring(st, d, k, True, 0).wait_recv()
                if st == 0:
                    copy_f(1, k - 1).wait_send()
                    copy_f(1, k).start()

        def block_step(j, carry2):
            d = lax.rem(j, 2)
            other = j // 2
            dist = k - other
            ok = (dist >= 0) & (dist <= FAR)
            ok = ok & ((d == 0) | ((dist >= 1) & (dist < FAR)))

            @pl.when(ok)
            def _():
                @pl.when(other == 1)
                def _():
                    dx = jnp.where(dist == FAR, 1, d)
                    land_f(dx, dist).wait_recv()

                accumulate(zblock(lax.rem(h + other, 2), d, dist))

            return carry2

        lax.fori_loop(0, 4, block_step, 0)
        return carry

    lax.fori_loop(0, FAR + 2, gather_step, 0)

    middle = rcopy(ms, mr, mid_sem.at[0], mid_sem.at[1], sib)

    @pl.when(c == 1)
    def _():
        ms[...] = pre[...].astype(BF)

    def gates():
        gap = jnp.sum(logit[...] * meta[...].astype(F32), axis=1, keepdims=True)
        return jax.nn.sigmoid(gap), jax.nn.sigmoid(-gap)

    @pl.when(c == 0)
    def _():
        gate, _ = gates()
        v = pre[...]
        ms[...] = (gate * (v * jax.nn.sigmoid(v))).astype(BF)

    middle.start()
    middle.wait_recv()

    @pl.when(c == 0)
    def _():
        gate, gate_other = gates()
        v = pre[...]
        u = mr[...].astype(F32)
        sg = jax.nn.sigmoid(v)
        pg[...] = (gate * u * (sg * (1.0 + v * (1.0 - sg)))).astype(BF)
        t = jnp.sum(v * sg * u, axis=1, keepdims=True) * gate * gate_other
        ts = t * meta[...].astype(F32)
        top = ts.astype(BF).astype(F32)
        lane = lax.broadcasted_iota(jnp.int32, (ROWS, 128), 1)
        tsb[...] = ts.astype(BF)
        tlb[...] = jnp.where(lane < NE, top, jnp.where(lane < 2 * NE, ts - top, 0.0)).astype(BF)

    def product(p, r):
        @pl.when(c == 0)
        def _():
            acc = dot_nt(pg[r, 0:HID], wu[0, lanes(p), :])
            acc += dot_nt(pg[r, HID : 2 * HID], wu[1, lanes(p), :])
            part[...] = acc + dot_nn(tsb[r, :], rt3[:, lanes(p)])

        @pl.when(c == 1)
        def _():
            acc = dot_nn(mr[r, 0:HID], wd[0, :, lanes(p)])
            part[...] = acc + dot_nn(mr[r, HID : 2 * HID], wd[1, :, lanes(p)])

    def tblock(hh, d, dist):
        return hh * NZ + zwrap(z + dist - 2 * d * dist)

    def sum_piece(d, far):
        return pl.ds(d * QUART, QUART) if far else pl.ds(0, HALF)

    def hop(st, d, t, far):
        rr = sum_piece(d, far)
        return rcopy(
            ring_s.at[st, d, t - 1, rr], ring_r.at[st, d, t - 1, rr], rs_ssem.at[st, d], rs_rsem.at[st, d, t - 1], znext(d)
        )

    def copy_rx(d, dist):
        return rcopy(xs.at[d, dist], xr.at[d, dist], rx_ssem.at[d], rx_rsem.at[d, dist], partner)

    plane = [(dh, dq) for dh in range(2) for dq in range(NE) if dh or dq]

    def plane_dev(dh, dq):
        return lax.rem(h + dh, 2), qwrap(q + dq)

    def copy_g1(i, dh, dq):
        hh, qq = plane_dev(dh, dq)
        return rcopy(gp.at[hh * NE + qq], g1.at[i], g1_ssem.at[0], g1_rsem.at[0], dev(hh, z, c, qq))

    def copy_g2(dz):
        return rcopy(g2s, g2.at[dz], g2_ssem.at[0], g2_rsem.at[0], dev(h, zwrap(z + dz), c, q))

    me_p = h * NE + q

    def copy_g3(i, dh, dq):
        hh, qq = plane_dev(dh, dq)
        return rcopy(g3s, g3.at[:, lanes(me_p)], g3_ssem.at[0], g3_rsem.at[0], dev(hh, z, c, qq))

    all_g1 = rcopy(g1, g1, g1_ssem.at[0], g1_rsem.at[0], sib)
    near_g2 = g2.at[pl.ds(1, NZ - 1)]
    all_g2 = rcopy(near_g2, near_g2, g2_ssem.at[0], g2_rsem.at[0], sib)
    all_g3 = rcopy(g1, g1, g3_ssem.at[0], g3_rsem.at[0], sib)

    g4 = rcopy(g3, gr_ref, g4_sem.at[0], g4_sem.at[1], sib)
    g4_own = pltpu.make_async_copy(g3, gr_ref, g4_sem.at[2])

    def router_stage(step):
        @pl.when((c == 0) & ((step == 1) | (step == 2)))
        def _():
            tl = tlb[...]

            def one(p, carry):
                full = dot_tn(tl, gath[p])
                gp[p] = full[0:NE] + full[NE : 2 * NE]
                return carry

            lax.fori_loop((step - 1) * (NBLK // 2), step * (NBLK // 2), one, 0)

        @pl.when((c == 0) & (step == 2))
        def _():
            for i, (dh, dq) in enumerate(plane):
                copy_g1(i, dh, dq).start()

        @pl.when((c == 0) & (step == FAR - 1))
        def _():
            total = gp[me_p]
            all_g1.wait_recv()
            for i in range(len(plane)):
                total = total + g1[i]
            g2s[...] = total
            for dz in range(1, NZ):
                copy_g2(dz).start()

        @pl.when((c == 0) & (step == FAR))
        def _():
            total = g2s[...]
            all_g2.wait_recv()
            for dz in range(1, NZ):
                total = total + g2[dz]
            g3s[...] = total
            g3[:, lanes(me_p)] = total
            for i, (dh, dq) in enumerate(plane):
                copy_g3(i, dh, dq).start()

        @pl.when((c == 0) & (step == FAR + 1))
        def _():
            all_g3.wait_recv()
            g4.start()
            g4_own.start()

    gu_own = pltpu.make_async_copy(gu0, gu_ref, gsem.at[0])
    gd_own = pltpu.make_async_copy(gd0, gd_ref, gsem.at[0])
    gu_give = rcopy(gu, gu_ref, gsem.at[1], gsem.at[2], sib)
    gd_give = rcopy(gd, gd_ref, gsem.at[1], gsem.at[2], sib)

    def weight_grads(step):
        def one(i, carry):
            p = (step - 1) * 4 + i

            @pl.when(c == 0)
            def _():
                full = dot_tn(gath[p], pg[...]).astype(BF)
                gu0[lanes(p), :] = full[:, 0:HID]
                gu[lanes(p), :] = full[:, HID : 2 * HID]

            @pl.when(c == 1)
            def _():
                full = dot_tn(mr[...], gath[p]).astype(BF)
                gd[:, lanes(p)] = full[0:HID]
                gd0[:, lanes(p)] = full[HID : 2 * HID]

            return carry

        @pl.when((step >= 1) & (step <= FAR))
        def _():
            lax.fori_loop(0, 4, one, 0)

        @pl.when((step == FAR) & (c == 0))
        def _():
            gu_own.start()
            gu_give.start()

        @pl.when((step == FAR) & (c == 1))
        def _():
            gd_own.start()
            gd_give.start()

    def ret_copy(kind, dy):
        qd = group(kind == 0, dy)
        sems = r_ssem.at[kind], r_rsem.at[kind]
        if kind == 2:
            return rcopy(fs1.at[rows_of(lax.rem(qd, NY))], ret1.at[rows_of(y)], *sems, dev(1 - h, z, c, qd))
        return rcopy(fs0.at[rows_of(qd)], ret0.at[rows_of(q)], *sems, dev(h, z, c, qd))

    def ret_all(kind):
        ref = rows_in(fs0, kind)
        return rcopy(ref, ref, r_ssem.at[kind], r_rsem.at[kind], sib)

    last = FAR + 1

    def scatter_step(step, carry):
        nxt = FAR - step

        def share(d, carry2):
            @pl.when(((step == 0) & (d == 1)) | ((step >= 1) & (step < FAR)) | ((step == FAR) & (d == 0)))
            def _():
                product(tblock(1 - h, d, nxt), second())
                xs[d, nxt] = part[...].astype(BF)

                @pl.when(step >= 1 + (1 - d))
                def _():
                    copy_rx(d, nxt + 1).wait_send()

                copy_rx(d, nxt).start()

            return carry2

        def stream(st, step):
            hh = 1 - h if st == 2 else h
            dist = last - step

            def one(d, carry2):
                @pl.when((((step == 1) | (step == last)) & (d == 0)) | ((step > 1) & (step < last)))
                def _():
                    product(tblock(hh, d, dist), second() if st == 0 else first())
                    total = part[...]
                    if st == 0:
                        far_d = jnp.where(step == 1, 1, d)
                        copy_rx(far_d, dist).wait_recv()
                        total = total + xr[far_d, dist].astype(F32)

                    @pl.when(step == 1)
                    def _():
                        for dd in range(2):
                            rr = slice(dd * QUART, (dd + 1) * QUART)
                            ring_s[st, dd, 0, rr] = total[rr].astype(BF)
                            hop(st, dd, 1, True).start()

                    @pl.when(step == 2)
                    def _():
                        hop(st, d, 1, True).wait_recv()
                        hop(st, d, 1, True).wait_send()
                        ring_s[st, d, 1] = total.astype(BF)
                        rr = pl.ds(d * QUART, QUART)
                        part[...] = total
                        got = part[rr, :] + ring_r[st, d, 0, rr, :].astype(F32)
                        ring_s[st, d, 1, rr, :] = got.astype(BF)
                        hop(st, d, 2, False).start()

                    @pl.when((step > 2) & (step < last))
                    def _():
                        hop(st, d, step - 1, False).wait_recv()
                        hop(st, d, step - 1, False).wait_send()
                        ring_s[st, d, step - 1] = (total + ring_r[st, d, step - 2].astype(F32)).astype(BF)
                        hop(st, d, step, False).start()

                    @pl.when(step == last)
                    def _():
                        hop(st, 0, FAR, False).wait_recv()
                        hop(st, 1, FAR, False).wait_recv()
                        got = total + ring_r[st, 0, FAR - 1].astype(F32) + ring_r[st, 1, FAR - 1].astype(F32)
                        if st == 2:
                            fs1[...] = got.astype(BF)
                        else:
                            fs0[second() if st == 0 else first(), :] = got.astype(BF)
                        for dy in range(NY):
                            if st == 0 and dy == 0:
                                ret0[rows_of(q), :] = fs0[rows_of(q), :]
                            else:
                                ret_copy(st, dy).start()

                return carry2

            lax.fori_loop(0, 2, one, 0)

        stream(1, step)

        @pl.when(step == FAR)
        def _():
            stream(0, step - 1)

        stream(2, step)
        lax.fori_loop(0, 2, share, 0)

        @pl.when(step == 1)
        def _():
            router_stage(step)
            weight_grads(step)

        stream(0, jnp.where(step < FAR, step - 1, step))

        @pl.when(step > 1)
        def _():
            router_stage(step)
            weight_grads(step)

        return carry

    lax.fori_loop(0, last + 1, scatter_step, 0)

    for kind in (1, 2, 0):
        ret_all(kind).wait_recv()
    got = dot_tn(pick[...], ret0[...]) + dot_tn(pick[first(), :], ret1[...])
    rounded = got.astype(BF)
    trade.wait_send()
    give[...] = dot_nt(rounded, place_other).astype(BF)
    give_tokens = rcopy(give, og_ref, o_sem.at[0], o_sem.at[1], sib)
    give_mixed = rcopy(give, om_ref, o_sem.at[0], o_sem.at[1], sib)
    put_tokens = pltpu.make_async_copy(keep, og_ref, o_sem.at[2])
    put_mixed = pltpu.make_async_copy(keep, om_ref, o_sem.at[2])

    @pl.when(c == 0)
    def _():
        give_tokens.start()

    @pl.when(c == 1)
    def _():
        give_mixed.start()

    keep[...] = dot_nt(rounded, place_mine).astype(BF)

    @pl.when(c == 0)
    def _():
        put_tokens.start()

    @pl.when(c == 1)
    def _():
        put_mixed.start()

    for kind in range(3):
        disp_all(kind).wait_send()
        ret_all(kind).wait_send()

    for d in range(2):
        for st in range(3):
            ring(st, d, FAR, True, 1).wait_send()
            hop(st, d, FAR, False).wait_send()
    copy_f(0, FAR - 1).wait_send()
    copy_f(1, FAR).wait_send()
    copy_rx(0, 0).wait_send()
    copy_rx(1, 1).wait_send()
    middle.wait_send()

    @pl.when(c == 0)
    def _():
        w_in_give.wait_send()
        meta_all.wait_send()
        all_g1.wait_send()
        all_g2.wait_send()
        all_g3.wait_send()
        g4.wait_send()
        g4_own.wait()
        gu_own.wait()
        gu_give.wait_send()
        gd_give.wait_recv()

    @pl.when(c == 1)
    def _():
        w_out_give.wait_send()
        g4.wait_recv()
        gd_own.wait()
        gd_give.wait_send()
        gu_give.wait_recv()

    @pl.when(c == 0)
    def _():
        put_tokens.wait()
        give_tokens.wait_send()
        give_mixed.wait_recv()

    @pl.when(c == 1)
    def _():
        put_mixed.wait()
        give_mixed.wait_send()
        give_tokens.wait_recv()


def vm(*shape, dtype=BF):
    return pltpu.VMEM(shape, dtype)


def dma(*shape):
    return pltpu.SemaphoreType.DMA(shape)


def store(om, og, gu, gd, gr, om_out, og_out, gu_out, gd_out, gr_out, sem):
    copies = [
        pltpu.make_async_copy(src, dst, sem.at[i])
        for i, (src, dst) in enumerate(((gu, gu_out), (gd, gd_out), (om, om_out), (og, og_out), (gr, gr_out)))
    ]
    for copy in copies:
        copy.start()
    for copy in copies:
        copy.wait()


def shards(tokens, expert_ids, slot_ids, router, up_weight, down_weight, cotangent):
    aspec = pl.BlockSpec(memory_space=pl.ANY)
    hspec = pl.BlockSpec(memory_space=pltpu.HBM)
    shapes = (
        jax.ShapeDtypeStruct((TOK, FEAT), BF),
        jax.ShapeDtypeStruct((TOK, FEAT), BF),
        jax.ShapeDtypeStruct((WIDTH, HID), BF),
        jax.ShapeDtypeStruct((HID, WIDTH), BF),
        jax.ShapeDtypeStruct((NE, WIDTH), F32),
    )
    results = pl.pallas_call(
        kernel,
        out_shape=(
            *shapes,
        ),
        in_specs=[hspec] * 7,
        out_specs=(aspec,) * 5,
        scratch_shapes=[
            vm(NBLK, ROWS, BLK), vm(2, WIDTH, HID), vm(2, HID, WIDTH), vm(WIDTH, HID), vm(HID, WIDTH), vm(WIDTH, HID), vm(HID, WIDTH),
            vm(128, WIDTH), vm(ROWS, TOK), vm(TOK, FEAT), vm(TOK, FEAT),
            vm(2, TOK, dtype=jnp.int32), vm(2, TOK, dtype=jnp.int32), vm(NE, WIDTH, dtype=F32),
            vm(TOK, FEAT), vm(ROWS, BLK), vm(ROWS, 128), vm(ROWS, 128),
            vm(ROWS, 2 * HID, dtype=F32), vm(ROWS, 128, dtype=F32), vm(ROWS, 2 * HID), vm(ROWS, 2 * HID),
            vm(ROWS, 2 * HID), vm(ROWS, 128), vm(ROWS, 128), vm(HALF, BLK, dtype=F32),
            vm(3, 2, FAR, HALF, BLK), vm(3, 2, FAR, HALF, BLK), vm(2, 5, HALF, BLK), vm(2, 5, HALF, BLK),
            vm(ROWS, BLK), vm(HALF, BLK), vm(ROWS, BLK), vm(HALF, BLK),
            vm(NBLK, NE, BLK, dtype=F32), vm(15, NE, BLK, dtype=F32), vm(NE, BLK, dtype=F32),
            vm(NZ, NE, BLK, dtype=F32), vm(NE, BLK, dtype=F32), vm(NE, WIDTH, dtype=F32),
            dma(5), dma(3), dma(2), dma(3), dma(3), dma(1), dma(1),
            dma(3, 2), dma(3, 2, FAR), dma(2), dma(2, 5), dma(2), dma(3, 2), dma(3, 2, FAR), dma(2), dma(2, 5),
            dma(3), dma(3), dma(3), dma(3),
            dma(1), dma(1), dma(1), dma(1), dma(1), dma(1), dma(3),
        ],
        compiler_params=pltpu.CompilerParams(
            collective_id=0, has_side_effects=True, vmem_limit_bytes=47 << 20
        ),
    )(
        *(
            pltpu.with_memory_space_constraint(v, pltpu.HBM)
            for v in (tokens, cotangent, expert_ids.T, slot_ids.T, router.T, up_weight[0], down_weight[0])
        )
    )
    mixed, grad_tokens, gu, gd, gr = pl.pallas_call(
        store,
        out_shape=shapes,
        in_specs=[aspec] * 5,
        out_specs=(hspec,) * 5,
        scratch_shapes=[dma(5)],
        compiler_params=pltpu.CompilerParams(vmem_limit_bytes=1 << 20),
    )(*results)
    return (mixed, grad_tokens, gu[None], gd[None], gr.T)


def solution(mesh):
    in_specs = (
        P("expert", "section"),
        P("expert", None),
        P("expert", None),
        P(),
        P("expert", None, "section"),
        P("expert", "section", None),
        P("expert", "section"),
    )
    out_specs = (
        P("expert", "section"),
        P("expert", "section"),
        P("expert", None, "section"),
        P("expert", "section", None),
        P(),
    )
    return jax.shard_map(shards, mesh=mesh, in_specs=in_specs, out_specs=out_specs, check_vma=False)
```

```python
import jax
import jax.numpy as jnp
from jax import lax
from jax.experimental import pallas as pl
from jax.experimental.pallas import tpu as pltpu
from jax.sharding import PartitionSpec as P

MESH = pl.DeviceIdType.MESH
NZ = 8
FAR = NZ // 2
NE = 8
CAP = 48
TOK = 192
FEAT = 192
BLK = 2 * FEAT
ROWS = NE * CAP
HALF = ROWS // 2
QUART = HALF // 2
HID = 256
WIDTH = 6144
NBLK = WIDTH // BLK
BF = jnp.bfloat16
F32 = jnp.float32
NY = NE // 2


def dot_nn(a, b):
    return jnp.dot(a, b, preferred_element_type=F32)


def dot_nt(a, b):
    return lax.dot_general(a, b, (((1,), (1,)), ((), ())), preferred_element_type=F32)


def dot_tn(a, b):
    return lax.dot_general(a, b, (((0,), (0,)), ((), ())), preferred_element_type=F32)


def lanes(p):
    return pl.ds(pl.multiple_of(p * BLK, BLK), BLK)


def rows_of(q):
    return pl.ds(pl.multiple_of(q * CAP, CAP), CAP)


def kernel(
    tok_ref, cot_ref, ids_hbm, slots_hbm, rt_hbm, up_ref, dn_ref,
    om_ref, og_ref, gu_ref, gd_ref, gr_ref,
    gath, wu, wd, gu, gd, gu0, gd0, rt3, pick, keep, give, ids_ref, slots_ref, rt_ref, xch, sent, msend, meta,
    pre, logit, ms, mr, pg, tsb, tlb, part,
    ring_s, ring_r, xs, xr,
    fs0, fs1, ret0, ret1,
    gp, g1, g2s, g2, g3s, g3,
    in_sem, w_sem, x_sem, d_ssem, d_rsem, m_ssem, m_rsem,
    ag_ssem, ag_rsem, f_ssem, f_rsem, mid_sem, rs_ssem, rs_rsem, rx_ssem, rx_rsem,
    gsem, r_ssem, r_rsem, o_sem,
    g1_ssem, g1_rsem, g2_ssem, g2_rsem, g3_ssem, g3_rsem, g4_sem,
):
    s = lax.axis_index("section")
    q = lax.axis_index("expert")
    c = lax.rem(s, 2)
    z = lax.rem(s // 2, NZ)
    h = s // (2 * NZ)

    def dev(hh, zz, cc, qq):
        return ((hh * NZ + zz) * 2 + cc, qq)

    def zwrap(v):
        return lax.rem(v + 2 * NZ, NZ)

    def qwrap(v):
        return lax.rem(v + NE, NE)

    lo_x = q // NY
    y = lax.rem(q, NY)

    def first(off=0, size=HALF):
        return pl.ds(pl.multiple_of((1 - lo_x) * HALF + off, QUART), size)

    def second(off=0, size=HALF):
        return pl.ds(pl.multiple_of(lo_x * HALF + off, QUART), size)

    def group(same, dy):
        return (lo_x if same else 1 - lo_x) * NY + lax.rem(y + NY + dy, NY)

    sib = dev(h, z, 1 - c, q)
    partner = dev(1 - h, z, c, q)

    def znext(d):
        return dev(h, zwrap(z + 1 - 2 * d), c, q)

    def rcopy(src, dst, ssem, rsem, target):
        return pltpu.make_async_remote_copy(
            src_ref=src, dst_ref=dst, send_sem=ssem, recv_sem=rsem, device_id=target, device_id_type=MESH
        )

    barrier = pltpu.get_barrier_semaphore()
    peers = [sib]
    for dh in range(2):
        for dq in range(NE):
            if dh or dq:
                peers.append(dev(lax.rem(h + dh, 2), z, c, qwrap(q + dq)))
    for dz in range(1, NZ):
        peers.append(dev(h, zwrap(z + dz), c, q))
    for peer in peers:
        pl.semaphore_signal(barrier, inc=1, device_id=peer, device_id_type=MESH)

    small = [
        pltpu.make_async_copy(ids_hbm, ids_ref, in_sem.at[0]),
        pltpu.make_async_copy(slots_hbm, slots_ref, in_sem.at[1]),
        pltpu.make_async_copy(rt_hbm, rt_ref, in_sem.at[2]),
    ]
    for copy in small:
        copy.start()
    tok_keep = pltpu.make_async_copy(tok_ref, keep, in_sem.at[3])
    cot_give = pltpu.make_async_copy(cot_ref, give, in_sem.at[4])
    cot_keep = pltpu.make_async_copy(cot_ref, keep, in_sem.at[3])
    tok_give = pltpu.make_async_copy(tok_ref, give, in_sem.at[4])
    w_in = pltpu.make_async_copy(up_ref, wu.at[0], w_sem.at[0])
    w_in_give = rcopy(dn_ref, wd.at[0], w_sem.at[1], w_sem.at[2], sib)
    w_out = pltpu.make_async_copy(dn_ref, wd.at[1], w_sem.at[0])
    w_out_give = rcopy(up_ref, wu.at[1], w_sem.at[1], w_sem.at[2], sib)

    @pl.when(c == 0)
    def _():
        cot_give.start()
        tok_keep.start()
        w_in.start()

    @pl.when(c == 1)
    def _():
        tok_give.start()
        cot_keep.start()
        w_out.start()

    @pl.when(c == 0)
    def _():
        cot_give.wait()
        tok_keep.wait()

    @pl.when(c == 1)
    def _():
        tok_give.wait()
        cot_keep.wait()

    pl.semaphore_wait(barrier, len(peers))
    trade = rcopy(give, xch, x_sem.at[0], x_sem.at[1], sib)
    trade.start()
    row = lax.broadcasted_iota(jnp.int32, (FEAT, BLK), 0)
    col = lax.broadcasted_iota(jnp.int32, (FEAT, BLK), 1)
    place_mine = (col == row + FEAT * c).astype(F32).astype(BF)
    place_other = (col == row + FEAT * (1 - c)).astype(F32).astype(BF)

    small[0].wait()
    small[1].wait()

    place0 = ids_ref[0:1, :] * CAP + slots_ref[0:1, :]
    place1 = ids_ref[1:2, :] * CAP + slots_ref[1:2, :]
    slot = lax.broadcasted_iota(jnp.int32, (ROWS, TOK), 0)
    hit0 = (slot == place0).astype(F32)
    hit1 = (slot == place1).astype(F32)
    pick[...] = (hit0 + hit1).astype(BF)
    half_both = dot_nn(keep[...], place_mine)
    trade.wait_recv()
    both = (half_both + dot_nn(xch[...], place_other)).astype(BF)
    sent[...] = dot_nn(pick[...], both).astype(BF)

    mine = h * NZ + z

    def disp(kind, dy):
        qd = group(kind == 0, dy)
        return rcopy(
            sent.at[rows_of(qd)], gath.at[mine, rows_of(q)], d_ssem.at[kind], d_rsem.at[kind],
            dev(1 - h if kind == 2 else h, z, c, qd),
        )

    def rows_in(ref, kind):
        return ref.at[pl.ds(0, (NY - 1 if kind == 0 else NY) * CAP)]

    def disp_all(kind):
        ref = rows_in(sent, kind)
        return rcopy(ref, ref, d_ssem.at[kind], d_rsem.at[kind], sib)

    def meta_copy(dq):
        qd = qwrap(q + dq)
        return rcopy(
            msend.at[rows_of(qd)], meta.at[rows_of(q)], m_ssem.at[0], m_rsem.at[0], dev(h, z, c, qd)
        )

    meta_all = rcopy(
        msend.at[pl.ds(0, ROWS - CAP)], msend.at[pl.ds(0, ROWS - CAP)], m_ssem.at[0], m_rsem.at[0], sib
    )

    plane_kinds = [(0, 2), (0, 1), (0, 3)] + [(kind, dy) for kind in (1, 2) for dy in (2, 1, 3, 0)]
    for kind, dy in plane_kinds:
        disp(kind, dy).start()

    gath[mine, rows_of(q), :] = sent[rows_of(q), :]

    lane8 = lax.broadcasted_iota(jnp.int32, (128, TOK), 0)
    expert = lax.rem(lane8, NE)
    live = lane8 < 3 * NE
    sign = jnp.where(live & (expert == ids_ref[0:1, :]), 1.0, 0.0) - jnp.where(
        live & (expert == ids_ref[1:2, :]), 1.0, 0.0
    )

    @pl.when(c == 0)
    def _():
        w_in_give.start()
        again = lax.broadcasted_iota(jnp.int32, (ROWS, TOK), 0)
        p0 = ids_ref[0:1, :] * CAP + slots_ref[0:1, :]
        p1 = ids_ref[1:2, :] * CAP + slots_ref[1:2, :]
        which = (again == p0).astype(F32) - (again == p1).astype(F32)
        msend[...] = dot_nt(which.astype(BF), sign.astype(BF)).astype(BF)
        for dq in range(1, NE):
            meta_copy(dq).start()
        meta[rows_of(q), :] = msend[rows_of(q), :]

    @pl.when(c == 1)
    def _():
        w_out_give.start()

    pre[...] = jnp.zeros((ROWS, 2 * HID), F32)
    logit[...] = jnp.zeros((ROWS, 128), F32)

    small[2].wait()

    def zblock(hh, d, k):
        return hh * NZ + zwrap(z - k + 2 * d * k)

    def piece(st, d, far):
        rows = second if st == 0 else first
        return rows(d * QUART, QUART) if far else rows()

    def ring(st, d, k, far, back):
        ref = gath.at[zblock(1 - h if st == 2 else h, d, k - back), piece(st, d, far)]
        return rcopy(ref, ref, ag_ssem.at[st, d], ag_rsem.at[st, d, k - 1], znext(d))

    def copy_f(d, k):
        ref = gath.at[zblock(h, d, k), second()]
        return rcopy(ref, ref, f_ssem.at[d], f_rsem.at[d, k], partner)

    def land_f(d, k):
        ref = gath.at[zblock(1 - h, d, k), second()]
        return rcopy(ref, ref, f_ssem.at[d], f_rsem.at[d, k], partner)

    disp_all(0).wait_recv()
    for d in range(2):
        ring(0, d, 1, False, 1).start()
    copy_f(0, 0).start()
    for st in (1, 2):
        disp_all(st).wait_recv()
        for d in range(2):
            ring(st, d, 1, False, 1).start()

    @pl.when(c == 0)
    def _():
        def split(p, carry):
            r = rt_ref[:, lanes(p)]
            top = r.astype(BF).astype(F32)
            mid = (r - top).astype(BF).astype(F32)
            low = r - top - mid
            rt3[:, lanes(p)] = jnp.concatenate([top, mid, low, jnp.zeros((104, BLK), F32)], axis=0).astype(BF)
            return carry

        lax.fori_loop(0, NBLK, split, 0)
        w_in.wait()
        w_out_give.wait_recv()
        meta_all.wait_recv()

    @pl.when(c == 1)
    def _():
        w_out.wait()
        w_in_give.wait_recv()

    def accumulate(p):
        @pl.when(c == 0)
        def _():
            x = gath[p]
            pre[:, 0:HID] += dot_nn(x, wu[0, lanes(p), :])
            pre[:, HID : 2 * HID] += dot_nn(x, wu[1, lanes(p), :])
            logit[...] += dot_nt(x, rt3[:, lanes(p)])

        @pl.when(c == 1)
        def _():
            x = gath[p]
            pre[:, 0:HID] += dot_nt(x, wd[0, :, lanes(p)])
            pre[:, HID : 2 * HID] += dot_nt(x, wd[1, :, lanes(p)])

    def gather_step(k, carry):
        @pl.when((k >= 1) & (k < FAR))
        def _():
            for st in range(3):
                for d in range(2):
                    ring(st, d, k, False, 0).wait_recv()
                    ring(st, d, k, False, 1).wait_send()

                    @pl.when(k < FAR - 1)
                    def _():
                        ring(st, d, k + 1, False, 1).start()

                    @pl.when(k == FAR - 1)
                    def _():
                        ring(st, d, k + 1, True, 1).start()

                    if st == 0:
                        if d == 0:
                            copy_f(0, k - 1).wait_send()
                        else:

                            @pl.when(k > 1)
                            def _():
                                copy_f(1, k - 1).wait_send()

                        copy_f(d, k).start()

        @pl.when(k == FAR)
        def _():
            for st in range(3):
                for d in range(2):
                    ring(st, d, k, True, 0).wait_recv()
                if st == 0:
                    copy_f(1, k - 1).wait_send()
                    copy_f(1, k).start()

        def block_step(j, carry2):
            d = lax.rem(j, 2)
            other = j // 2
            dist = k - other
            ok = (dist >= 0) & (dist <= FAR)
            ok = ok & ((d == 0) | ((dist >= 1) & (dist < FAR)))

            @pl.when(ok)
            def _():
                @pl.when(other == 1)
                def _():
                    dx = jnp.where(dist == FAR, 1, d)
                    land_f(dx, dist).wait_recv()

                accumulate(zblock(lax.rem(h + other, 2), d, dist))

            return carry2

        lax.fori_loop(0, 4, block_step, 0)
        return carry

    lax.fori_loop(0, FAR + 2, gather_step, 0)

    middle = rcopy(ms, mr, mid_sem.at[0], mid_sem.at[1], sib)

    @pl.when(c == 1)
    def _():
        ms[...] = pre[...].astype(BF)

    def gates():
        gap = jnp.sum(logit[...] * meta[...].astype(F32), axis=1, keepdims=True)
        return jax.nn.sigmoid(gap), jax.nn.sigmoid(-gap)

    @pl.when(c == 0)
    def _():
        gate, _ = gates()
        v = pre[...]
        ms[...] = (gate * (v * jax.nn.sigmoid(v))).astype(BF)

    middle.start()
    middle.wait_recv()

    @pl.when(c == 0)
    def _():
        gate, gate_other = gates()
        v = pre[...]
        u = mr[...].astype(F32)
        sg = jax.nn.sigmoid(v)
        pg[...] = (gate * u * (sg * (1.0 + v * (1.0 - sg)))).astype(BF)
        t = jnp.sum(v * sg * u, axis=1, keepdims=True) * gate * gate_other
        ts = t * meta[...].astype(F32)
        top = ts.astype(BF).astype(F32)
        lane = lax.broadcasted_iota(jnp.int32, (ROWS, 128), 1)
        tsb[...] = ts.astype(BF)
        tlb[...] = jnp.where(lane < NE, top, jnp.where(lane < 2 * NE, ts - top, 0.0)).astype(BF)

    def product(p, r):
        @pl.when(c == 0)
        def _():
            acc = dot_nt(pg[r, 0:HID], wu[0, lanes(p), :])
            acc += dot_nt(pg[r, HID : 2 * HID], wu[1, lanes(p), :])
            part[...] = acc + dot_nn(tsb[r, :], rt3[:, lanes(p)])

        @pl.when(c == 1)
        def _():
            acc = dot_nn(mr[r, 0:HID], wd[0, :, lanes(p)])
            part[...] = acc + dot_nn(mr[r, HID : 2 * HID], wd[1, :, lanes(p)])

    def tblock(hh, d, dist):
        return hh * NZ + zwrap(z + dist - 2 * d * dist)

    def sum_piece(d, far):
        return pl.ds(d * QUART, QUART) if far else pl.ds(0, HALF)

    def hop(st, d, t, far):
        rr = sum_piece(d, far)
        return rcopy(
            ring_s.at[st, d, t - 1, rr], ring_r.at[st, d, t - 1, rr], rs_ssem.at[st, d], rs_rsem.at[st, d, t - 1], znext(d)
        )

    def copy_rx(d, dist):
        return rcopy(xs.at[d, dist], xr.at[d, dist], rx_ssem.at[d, dist], rx_rsem.at[d, dist], partner)

    plane = [(dh, dq) for dh in range(2) for dq in range(NE) if dh or dq]

    def plane_dev(dh, dq):
        return lax.rem(h + dh, 2), qwrap(q + dq)

    def copy_g1(i, dh, dq):
        hh, qq = plane_dev(dh, dq)
        return rcopy(gp.at[hh * NE + qq], g1.at[i], g1_ssem.at[0], g1_rsem.at[0], dev(hh, z, c, qq))

    def copy_g2(dz):
        return rcopy(g2s, g2.at[dz], g2_ssem.at[0], g2_rsem.at[0], dev(h, zwrap(z + dz), c, q))

    me_p = h * NE + q

    def copy_g3(i, dh, dq):
        hh, qq = plane_dev(dh, dq)
        return rcopy(g3s, g3.at[:, lanes(me_p)], g3_ssem.at[0], g3_rsem.at[0], dev(hh, z, c, qq))

    all_g1 = rcopy(g1, g1, g1_ssem.at[0], g1_rsem.at[0], sib)
    near_g2 = g2.at[pl.ds(1, NZ - 1)]
    all_g2 = rcopy(near_g2, near_g2, g2_ssem.at[0], g2_rsem.at[0], sib)
    all_g3 = rcopy(g1, g1, g3_ssem.at[0], g3_rsem.at[0], sib)

    g4 = rcopy(g3, gr_ref, g4_sem.at[0], g4_sem.at[1], sib)
    g4_own = pltpu.make_async_copy(g3, gr_ref, g4_sem.at[2])

    def router_parts():
        tl = tlb[...]

        def one(p, carry):
            full = dot_tn(tl, gath[p])
            gp[p] = full[0:NE] + full[NE : 2 * NE]
            return carry

        lax.fori_loop(0, NBLK, one, 0)
        for i, (dh, dq) in enumerate(plane):
            copy_g1(i, dh, dq).start()

    def router_plane():
        all_g1.wait_recv()
        total = gp[me_p]
        for i in range(len(plane)):
            total = total + g1[i]
        g2s[...] = total
        for dz in range(1, NZ):
            copy_g2(dz).start()

    def router_column():
        all_g2.wait_recv()
        total = g2s[...]
        for dz in range(1, NZ):
            total = total + g2[dz]
        g3s[...] = total
        g3[:, lanes(me_p)] = total
        for i, (dh, dq) in enumerate(plane):
            copy_g3(i, dh, dq).start()

    def router_out():
        all_g3.wait_recv()
        g4.start()
        g4_own.start()

    gu_own = pltpu.make_async_copy(gu0, gu_ref, gsem.at[0])
    gd_own = pltpu.make_async_copy(gd0, gd_ref, gsem.at[0])
    gu_give = rcopy(gu, gu_ref, gsem.at[1], gsem.at[2], sib)
    gd_give = rcopy(gd, gd_ref, gsem.at[1], gsem.at[2], sib)

    def weight_grads(step):
        def one(p, carry):
            @pl.when(c == 0)
            def _():
                full = dot_tn(gath[p], pg[...]).astype(BF)
                gu0[lanes(p), :] = full[:, 0:HID]
                gu[lanes(p), :] = full[:, HID : 2 * HID]

            @pl.when(c == 1)
            def _():
                full = dot_tn(mr[...], gath[p]).astype(BF)
                gd[:, lanes(p)] = full[0:HID]
                gd0[:, lanes(p)] = full[HID : 2 * HID]

            return carry

        begin = jnp.where(step == 1, 0, jnp.where(step == FAR - 1, 4, 10))
        end = jnp.where(step == 1, 4, jnp.where(step == FAR - 1, 10, NBLK))

        @pl.when((step == 1) | (step == FAR - 1) | (step == FAR))
        def _():
            lax.fori_loop(begin, end, one, 0)

        @pl.when((step == FAR) & (c == 0))
        def _():
            gu_own.start()
            gu_give.start()

        @pl.when((step == FAR) & (c == 1))
        def _():
            gd_own.start()
            gd_give.start()

    def ret_copy(kind, dy):
        qd = group(kind == 0, dy)
        sems = r_ssem.at[kind], r_rsem.at[kind]
        if kind == 2:
            return rcopy(fs1.at[rows_of(lax.rem(qd, NY))], ret1.at[rows_of(y)], *sems, dev(1 - h, z, c, qd))
        return rcopy(fs0.at[rows_of(qd)], ret0.at[rows_of(q)], *sems, dev(h, z, c, qd))

    def ret_all(kind):
        ref = rows_in(fs0, kind)
        return rcopy(ref, ref, r_ssem.at[kind], r_rsem.at[kind], sib)

    last = FAR + 1

    def scatter_step(step, carry):
        nxt = FAR - step

        def share(d, carry2):
            @pl.when(((step == 0) & (d == 1)) | ((step >= 1) & (step < FAR)) | ((step == FAR) & (d == 0)))
            def _():
                product(tblock(1 - h, d, nxt), second())
                xs[d, nxt] = part[...].astype(BF)
                copy_rx(d, nxt).start()

            return carry2

        def stream(st, step):
            hh = 1 - h if st == 2 else h
            dist = last - step

            def one(d, carry2):
                @pl.when((((step == 1) | (step == last)) & (d == 0)) | ((step > 1) & (step < last)))
                def _():
                    product(tblock(hh, d, dist), second() if st == 0 else first())
                    total = part[...]
                    if st == 0:
                        far_d = jnp.where(step == 1, 1, d)
                        copy_rx(far_d, dist).wait_recv()
                        total = total + xr[far_d, dist].astype(F32)

                    @pl.when(step == 1)
                    def _():
                        for dd in range(2):
                            rr = slice(dd * QUART, (dd + 1) * QUART)
                            ring_s[st, dd, 0, rr] = total[rr].astype(BF)
                            hop(st, dd, 1, True).start()

                    @pl.when(step == 2)
                    def _():
                        hop(st, d, 1, True).wait_recv()
                        hop(st, d, 1, True).wait_send()
                        ring_s[st, d, 1] = total.astype(BF)
                        rr = pl.ds(d * QUART, QUART)
                        part[...] = total
                        got = part[rr, :] + ring_r[st, d, 0, rr, :].astype(F32)
                        ring_s[st, d, 1, rr, :] = got.astype(BF)
                        hop(st, d, 2, False).start()

                    @pl.when((step > 2) & (step < last))
                    def _():
                        hop(st, d, step - 1, False).wait_recv()
                        hop(st, d, step - 1, False).wait_send()
                        ring_s[st, d, step - 1] = (total + ring_r[st, d, step - 2].astype(F32)).astype(BF)
                        hop(st, d, step, False).start()

                    @pl.when(step == last)
                    def _():
                        hop(st, 0, FAR, False).wait_recv()
                        hop(st, 1, FAR, False).wait_recv()
                        got = total + ring_r[st, 0, FAR - 1].astype(F32) + ring_r[st, 1, FAR - 1].astype(F32)
                        if st == 2:
                            fs1[...] = got.astype(BF)
                        else:
                            fs0[second() if st == 0 else first(), :] = got.astype(BF)
                        for dy in range(NY):
                            if st == 0 and dy == 0:
                                ret0[rows_of(q), :] = fs0[rows_of(q), :]
                            else:
                                ret_copy(st, dy).start()

                return carry2

            lax.fori_loop(0, 2, one, 0)

        stream(1, step)

        @pl.when(step == FAR)
        def _():
            @pl.when(c == 0)
            def _():
                router_plane()

            stream(0, step - 1)

        stream(2, step)
        lax.fori_loop(0, 2, share, 0)
        stream(0, jnp.where(step < FAR, step - 1, step))

        @pl.when((step == 2) & (c == 0))
        def _():
            router_parts()

        @pl.when((step == FAR) & (c == 0))
        def _():
            router_column()

        weight_grads(step)
        return carry

    lax.fori_loop(0, last + 1, scatter_step, 0)

    for kind in (1, 2):
        ret_all(kind).wait_recv()
    got = dot_tn(pick[first(), :], ret0[first(), :]) + dot_tn(pick[first(), :], ret1[...])
    ret_all(0).wait_recv()
    got = got + dot_tn(pick[second(), :], ret0[second(), :])
    rounded = got.astype(BF)
    trade.wait_send()
    give[...] = dot_nt(rounded, place_other).astype(BF)
    give_tokens = rcopy(give, og_ref, o_sem.at[0], o_sem.at[1], sib)
    give_mixed = rcopy(give, om_ref, o_sem.at[0], o_sem.at[1], sib)
    put_tokens = pltpu.make_async_copy(keep, og_ref, o_sem.at[2])
    put_mixed = pltpu.make_async_copy(keep, om_ref, o_sem.at[2])

    @pl.when(c == 0)
    def _():
        give_tokens.start()

    @pl.when(c == 1)
    def _():
        give_mixed.start()

    keep[...] = dot_nt(rounded, place_mine).astype(BF)

    @pl.when(c == 0)
    def _():
        put_tokens.start()
        router_out()

    @pl.when(c == 1)
    def _():
        put_mixed.start()

    for kind in range(3):
        disp_all(kind).wait_send()
        ret_all(kind).wait_send()

    for d in range(2):
        for st in range(3):
            ring(st, d, FAR, True, 1).wait_send()
            hop(st, d, FAR, False).wait_send()
    copy_f(0, FAR - 1).wait_send()
    copy_f(1, FAR).wait_send()
    for k in range(FAR):
        copy_rx(0, k).wait_send()
        copy_rx(1, k + 1).wait_send()
    middle.wait_send()

    @pl.when(c == 0)
    def _():
        w_in_give.wait_send()
        meta_all.wait_send()
        all_g1.wait_send()
        all_g2.wait_send()
        all_g3.wait_send()
        g4.wait_send()
        g4_own.wait()
        gu_own.wait()
        gu_give.wait_send()
        gd_give.wait_recv()

    @pl.when(c == 1)
    def _():
        w_out_give.wait_send()
        g4.wait_recv()
        gd_own.wait()
        gd_give.wait_send()
        gu_give.wait_recv()

    @pl.when(c == 0)
    def _():
        put_tokens.wait()
        give_tokens.wait_send()
        give_mixed.wait_recv()

    @pl.when(c == 1)
    def _():
        put_mixed.wait()
        give_mixed.wait_send()
        give_tokens.wait_recv()


def vm(*shape, dtype=BF):
    return pltpu.VMEM(shape, dtype)


def dma(*shape):
    return pltpu.SemaphoreType.DMA(shape)


def store(om, og, gu, gd, gr, om_out, og_out, gu_out, gd_out, gr_out, sem):
    copies = [
        pltpu.make_async_copy(src, dst, sem.at[i])
        for i, (src, dst) in enumerate(((gu, gu_out), (gd, gd_out), (om, om_out), (og, og_out), (gr, gr_out)))
    ]
    for copy in copies:
        copy.start()
    for copy in copies:
        copy.wait()


def shards(tokens, expert_ids, slot_ids, router, up_weight, down_weight, cotangent):
    aspec = pl.BlockSpec(memory_space=pl.ANY)
    hspec = pl.BlockSpec(memory_space=pltpu.HBM)
    shapes = (
        jax.ShapeDtypeStruct((TOK, FEAT), BF),
        jax.ShapeDtypeStruct((TOK, FEAT), BF),
        jax.ShapeDtypeStruct((WIDTH, HID), BF),
        jax.ShapeDtypeStruct((HID, WIDTH), BF),
        jax.ShapeDtypeStruct((NE, WIDTH), F32),
    )
    results = pl.pallas_call(
        kernel,
        out_shape=(
            *shapes,
        ),
        in_specs=[hspec] * 7,
        out_specs=(aspec,) * 5,
        scratch_shapes=[
            vm(NBLK, ROWS, BLK), vm(2, WIDTH, HID), vm(2, HID, WIDTH), vm(WIDTH, HID), vm(HID, WIDTH), vm(WIDTH, HID), vm(HID, WIDTH),
            vm(128, WIDTH), vm(ROWS, TOK), vm(TOK, FEAT), vm(TOK, FEAT),
            vm(2, TOK, dtype=jnp.int32), vm(2, TOK, dtype=jnp.int32), vm(NE, WIDTH, dtype=F32),
            vm(TOK, FEAT), vm(ROWS, BLK), vm(ROWS, 128), vm(ROWS, 128),
            vm(ROWS, 2 * HID, dtype=F32), vm(ROWS, 128, dtype=F32), vm(ROWS, 2 * HID), vm(ROWS, 2 * HID),
            vm(ROWS, 2 * HID), vm(ROWS, 128), vm(ROWS, 128), vm(HALF, BLK, dtype=F32),
            vm(3, 2, FAR, HALF, BLK), vm(3, 2, FAR, HALF, BLK), vm(2, 5, HALF, BLK), vm(2, 5, HALF, BLK),
            vm(ROWS, BLK), vm(HALF, BLK), vm(ROWS, BLK), vm(HALF, BLK),
            vm(NBLK, NE, BLK, dtype=F32), vm(15, NE, BLK, dtype=F32), vm(NE, BLK, dtype=F32),
            vm(NZ, NE, BLK, dtype=F32), vm(NE, BLK, dtype=F32), vm(NE, WIDTH, dtype=F32),
            dma(5), dma(3), dma(2), dma(3), dma(3), dma(1), dma(1),
            dma(3, 2), dma(3, 2, FAR), dma(2), dma(2, 5), dma(2), dma(3, 2), dma(3, 2, FAR), dma(2, 5), dma(2, 5),
            dma(3), dma(3), dma(3), dma(3),
            dma(1), dma(1), dma(1), dma(1), dma(1), dma(1), dma(3),
        ],
        compiler_params=pltpu.CompilerParams(
            collective_id=0, has_side_effects=True, vmem_limit_bytes=47 << 20
        ),
    )(
        *(
            pltpu.with_memory_space_constraint(v, pltpu.HBM)
            for v in (tokens, cotangent, expert_ids.T, slot_ids.T, router.T, up_weight[0], down_weight[0])
        )
    )
    mixed, grad_tokens, gu, gd, gr = pl.pallas_call(
        store,
        out_shape=shapes,
        in_specs=[aspec] * 5,
        out_specs=(hspec,) * 5,
        scratch_shapes=[dma(5)],
        compiler_params=pltpu.CompilerParams(vmem_limit_bytes=1 << 20),
    )(*results)
    return (mixed, grad_tokens, gu[None], gd[None], gr.T)


def solution(mesh):
    in_specs = (
        P("expert", "section"),
        P("expert", None),
        P("expert", None),
        P(),
        P("expert", None, "section"),
        P("expert", "section", None),
        P("expert", "section"),
    )
    out_specs = (
        P("expert", "section"),
        P("expert", "section"),
        P("expert", None, "section"),
        P("expert", "section", None),
        P(),
    )
    return jax.shard_map(shards, mesh=mesh, in_specs=in_specs, out_specs=out_specs, check_vma=False)
```

```python
import jax
import jax.numpy as jnp
from jax import lax
from jax.experimental import pallas as pl
from jax.experimental.pallas import tpu as pltpu
from jax.sharding import PartitionSpec as P

MESH = pl.DeviceIdType.MESH
NZ = 8
FAR = NZ // 2
NE = 8
CAP = 48
TOK = 192
FEAT = 192
BLK = 2 * FEAT
ROWS = NE * CAP
HALF = ROWS // 2
QUART = HALF // 2
HID = 256
WIDTH = 6144
NBLK = WIDTH // BLK
BF = jnp.bfloat16
F32 = jnp.float32
NY = NE // 2


def dot_nn(a, b):
    return jnp.dot(a, b, preferred_element_type=F32)


def dot_nt(a, b):
    return lax.dot_general(a, b, (((1,), (1,)), ((), ())), preferred_element_type=F32)


def dot_tn(a, b):
    return lax.dot_general(a, b, (((0,), (0,)), ((), ())), preferred_element_type=F32)


def lanes(p):
    return pl.ds(pl.multiple_of(p * BLK, BLK), BLK)


def rows_of(q):
    return pl.ds(pl.multiple_of(q * CAP, CAP), CAP)


def kernel(
    tok_ref, cot_ref, ids_hbm, slots_hbm, rt_hbm, up_ref, dn_ref,
    om_ref, og_ref, gu_ref, gd_ref, gr_ref,
    gath, wu, wd, gu, gd, gu0, gd0, rt3, pick, keep, give, ids_ref, slots_ref, rt_ref, xch, sent, msend, meta,
    pre, logit, ms, mr, pg, tsb, tlb, part,
    ring_s, ring_r, xs, xr,
    fs0, fs1, ret0, ret1,
    gp, g1, g2s, g2, g3s, g3,
    in_sem, w_sem, x_sem, d_ssem, d_rsem, m_ssem, m_rsem,
    ag_ssem, ag_rsem, f_ssem, f_rsem, mid_sem, rs_ssem, rs_rsem, rx_ssem, rx_rsem,
    gsem, r_ssem, r_rsem, o_sem,
    g1_ssem, g1_rsem, g2_ssem, g2_rsem, g3_ssem, g3_rsem, g4_sem,
):
    s = lax.axis_index("section")
    q = lax.axis_index("expert")
    c = lax.rem(s, 2)
    z = lax.rem(s // 2, NZ)
    h = s // (2 * NZ)

    def dev(hh, zz, cc, qq):
        return ((hh * NZ + zz) * 2 + cc, qq)

    def zwrap(v):
        return lax.rem(v + 2 * NZ, NZ)

    def qwrap(v):
        return lax.rem(v + NE, NE)

    lo_x = q // NY
    y = lax.rem(q, NY)

    def first(off=0, size=HALF):
        return pl.ds(pl.multiple_of((1 - lo_x) * HALF + off, QUART), size)

    def second(off=0, size=HALF):
        return pl.ds(pl.multiple_of(lo_x * HALF + off, QUART), size)

    def group(same, dy):
        return (lo_x if same else 1 - lo_x) * NY + lax.rem(y + NY + dy, NY)

    sib = dev(h, z, 1 - c, q)
    partner = dev(1 - h, z, c, q)

    def znext(d):
        return dev(h, zwrap(z + 1 - 2 * d), c, q)

    def rcopy(src, dst, ssem, rsem, target):
        return pltpu.make_async_remote_copy(
            src_ref=src, dst_ref=dst, send_sem=ssem, recv_sem=rsem, device_id=target, device_id_type=MESH
        )

    barrier = pltpu.get_barrier_semaphore()
    peers = [sib]
    for dh in range(2):
        for dq in range(NE):
            if dh or dq:
                peers.append(dev(lax.rem(h + dh, 2), z, c, qwrap(q + dq)))
    for dz in range(1, NZ):
        peers.append(dev(h, zwrap(z + dz), c, q))
    for peer in peers:
        pl.semaphore_signal(barrier, inc=1, device_id=peer, device_id_type=MESH)

    small = [
        pltpu.make_async_copy(ids_hbm, ids_ref, in_sem.at[0]),
        pltpu.make_async_copy(slots_hbm, slots_ref, in_sem.at[1]),
        pltpu.make_async_copy(rt_hbm, rt_ref, in_sem.at[2]),
    ]
    for copy in small:
        copy.start()
    tok_keep = pltpu.make_async_copy(tok_ref, keep, in_sem.at[3])
    cot_keep = pltpu.make_async_copy(cot_ref, keep, in_sem.at[3])
    w_in = pltpu.make_async_copy(up_ref, wu.at[0], w_sem.at[0])
    w_in_give = rcopy(dn_ref, wd.at[0], w_sem.at[1], w_sem.at[2], sib)
    w_out = pltpu.make_async_copy(dn_ref, wd.at[1], w_sem.at[0])
    w_out_give = rcopy(up_ref, wu.at[1], w_sem.at[1], w_sem.at[2], sib)

    @pl.when(c == 0)
    def _():
        tok_keep.start()
        w_in.start()

    @pl.when(c == 1)
    def _():
        cot_keep.start()
        w_out.start()

    pl.semaphore_wait(barrier, len(peers))
    trade = rcopy(cot_ref, xch, x_sem.at[0], x_sem.at[1], sib)
    trade_back = rcopy(tok_ref, xch, x_sem.at[0], x_sem.at[1], sib)

    @pl.when(c == 0)
    def _():
        trade.start()
        tok_keep.wait()

    @pl.when(c == 1)
    def _():
        trade_back.start()
        cot_keep.wait()

    row = lax.broadcasted_iota(jnp.int32, (FEAT, BLK), 0)
    col = lax.broadcasted_iota(jnp.int32, (FEAT, BLK), 1)
    place_mine = (col == row + FEAT * c).astype(F32).astype(BF)
    place_other = (col == row + FEAT * (1 - c)).astype(F32).astype(BF)

    small[0].wait()
    small[1].wait()

    place0 = ids_ref[0:1, :] * CAP + slots_ref[0:1, :]
    place1 = ids_ref[1:2, :] * CAP + slots_ref[1:2, :]
    slot = lax.broadcasted_iota(jnp.int32, (ROWS, TOK), 0)
    hit0 = (slot == place0).astype(F32)
    hit1 = (slot == place1).astype(F32)
    pick[...] = (hit0 + hit1).astype(BF)
    half_both = dot_nn(keep[...], place_mine)
    trade.wait_recv()
    both = (half_both + dot_nn(xch[...], place_other)).astype(BF)
    sent[...] = dot_nn(pick[...], both).astype(BF)

    mine = h * NZ + z

    def disp(kind, dy):
        qd = group(kind == 0, dy)
        return rcopy(
            sent.at[rows_of(qd)], gath.at[mine, rows_of(q)], d_ssem.at[kind], d_rsem.at[kind],
            dev(1 - h if kind == 2 else h, z, c, qd),
        )

    def rows_in(ref, kind):
        return ref.at[pl.ds(0, (NY - 1 if kind == 0 else NY) * CAP)]

    def disp_all(kind):
        ref = rows_in(sent, kind)
        return rcopy(ref, ref, d_ssem.at[kind], d_rsem.at[kind], sib)

    def meta_copy(dq):
        qd = qwrap(q + dq)
        return rcopy(
            msend.at[rows_of(qd)], meta.at[rows_of(q)], m_ssem.at[0], m_rsem.at[0], dev(h, z, c, qd)
        )

    meta_all = rcopy(
        msend.at[pl.ds(0, ROWS - CAP)], msend.at[pl.ds(0, ROWS - CAP)], m_ssem.at[0], m_rsem.at[0], sib
    )

    plane_kinds = [(0, 2), (0, 1), (0, 3)] + [(kind, dy) for kind in (1, 2) for dy in (2, 1, 3, 0)]
    for kind, dy in plane_kinds:
        disp(kind, dy).start()

    gath[mine, rows_of(q), :] = sent[rows_of(q), :]

    lane8 = lax.broadcasted_iota(jnp.int32, (128, TOK), 0)
    expert = lax.rem(lane8, NE)
    live = lane8 < 3 * NE
    sign = jnp.where(live & (expert == ids_ref[0:1, :]), 1.0, 0.0) - jnp.where(
        live & (expert == ids_ref[1:2, :]), 1.0, 0.0
    )

    @pl.when(c == 0)
    def _():
        w_in_give.start()
        again = lax.broadcasted_iota(jnp.int32, (ROWS, TOK), 0)
        p0 = ids_ref[0:1, :] * CAP + slots_ref[0:1, :]
        p1 = ids_ref[1:2, :] * CAP + slots_ref[1:2, :]
        which = (again == p0).astype(F32) - (again == p1).astype(F32)
        msend[...] = dot_nt(which.astype(BF), sign.astype(BF)).astype(BF)
        for dq in range(1, NE):
            meta_copy(dq).start()
        meta[rows_of(q), :] = msend[rows_of(q), :]

    @pl.when(c == 1)
    def _():
        w_out_give.start()

    pre[...] = jnp.zeros((ROWS, 2 * HID), F32)
    logit[...] = jnp.zeros((ROWS, 128), F32)

    small[2].wait()

    def zblock(hh, d, k):
        return hh * NZ + zwrap(z - k + 2 * d * k)

    def piece(st, d, far):
        rows = second if st == 0 else first
        return rows(d * QUART, QUART) if far else rows()

    def ring(st, d, k, far, back):
        ref = gath.at[zblock(1 - h if st == 2 else h, d, k - back), piece(st, d, far)]
        return rcopy(ref, ref, ag_ssem.at[st, d], ag_rsem.at[st, d, k - 1], znext(d))

    def copy_f(d, k):
        ref = gath.at[zblock(h, d, k), second()]
        return rcopy(ref, ref, f_ssem.at[d], f_rsem.at[d, k], partner)

    def land_f(d, k):
        ref = gath.at[zblock(1 - h, d, k), second()]
        return rcopy(ref, ref, f_ssem.at[d], f_rsem.at[d, k], partner)

    disp_all(0).wait_recv()
    for d in range(2):
        ring(0, d, 1, False, 1).start()
    copy_f(0, 0).start()
    for st in (1, 2):
        disp_all(st).wait_recv()
        for d in range(2):
            ring(st, d, 1, False, 1).start()

    @pl.when(c == 0)
    def _():
        def split(p, carry):
            r = rt_ref[:, lanes(p)]
            top = r.astype(BF).astype(F32)
            mid = (r - top).astype(BF).astype(F32)
            low = r - top - mid
            rt3[:, lanes(p)] = jnp.concatenate([top, mid, low, jnp.zeros((104, BLK), F32)], axis=0).astype(BF)
            return carry

        lax.fori_loop(0, NBLK, split, 0)
        w_in.wait()
        w_out_give.wait_recv()
        meta_all.wait_recv()

    @pl.when(c == 1)
    def _():
        w_out.wait()
        w_in_give.wait_recv()

    def accumulate(p):
        @pl.when(c == 0)
        def _():
            x = gath[p]
            pre[:, 0:HID] += dot_nn(x, wu[0, lanes(p), :])
            pre[:, HID : 2 * HID] += dot_nn(x, wu[1, lanes(p), :])
            logit[...] += dot_nt(x, rt3[:, lanes(p)])

        @pl.when(c == 1)
        def _():
            x = gath[p]
            pre[:, 0:HID] += dot_nt(x, wd[0, :, lanes(p)])
            pre[:, HID : 2 * HID] += dot_nt(x, wd[1, :, lanes(p)])

    def gather_step(k, carry):
        @pl.when((k >= 1) & (k < FAR))
        def _():
            for st in range(3):
                for d in range(2):
                    ring(st, d, k, False, 0).wait_recv()
                    ring(st, d, k, False, 1).wait_send()

                    @pl.when(k < FAR - 1)
                    def _():
                        ring(st, d, k + 1, False, 1).start()

                    @pl.when(k == FAR - 1)
                    def _():
                        ring(st, d, k + 1, True, 1).start()

                    if st == 0:
                        if d == 0:
                            copy_f(0, k - 1).wait_send()
                        else:

                            @pl.when(k > 1)
                            def _():
                                copy_f(1, k - 1).wait_send()

                        copy_f(d, k).start()

        @pl.when(k == FAR)
        def _():
            for st in range(3):
                for d in range(2):
                    ring(st, d, k, True, 0).wait_recv()
                if st == 0:
                    copy_f(1, k - 1).wait_send()
                    copy_f(1, k).start()

        def block_step(j, carry2):
            d = lax.rem(j, 2)
            other = j // 2
            dist = k - other
            ok = (dist >= 0) & (dist <= FAR)
            ok = ok & ((d == 0) | ((dist >= 1) & (dist < FAR)))

            @pl.when(ok)
            def _():
                @pl.when(other == 1)
                def _():
                    dx = jnp.where(dist == FAR, 1, d)
                    land_f(dx, dist).wait_recv()

                accumulate(zblock(lax.rem(h + other, 2), d, dist))

            return carry2

        lax.fori_loop(0, 4, block_step, 0)
        return carry

    lax.fori_loop(0, FAR + 2, gather_step, 0)

    middle = rcopy(ms, mr, mid_sem.at[0], mid_sem.at[1], sib)

    @pl.when(c == 1)
    def _():
        ms[...] = pre[...].astype(BF)

    def gates():
        gap = jnp.sum(logit[...] * meta[...].astype(F32), axis=1, keepdims=True)
        return jax.nn.sigmoid(gap), jax.nn.sigmoid(-gap)

    @pl.when(c == 0)
    def _():
        gate, _ = gates()
        v = pre[...]
        ms[...] = (gate * (v * jax.nn.sigmoid(v))).astype(BF)

    middle.start()
    middle.wait_recv()

    @pl.when(c == 0)
    def _():
        gate, gate_other = gates()
        v = pre[...]
        u = mr[...].astype(F32)
        sg = jax.nn.sigmoid(v)
        pg[...] = (gate * u * (sg * (1.0 + v * (1.0 - sg)))).astype(BF)
        t = jnp.sum(v * sg * u, axis=1, keepdims=True) * gate * gate_other
        ts = t * meta[...].astype(F32)
        top = ts.astype(BF).astype(F32)
        lane = lax.broadcasted_iota(jnp.int32, (ROWS, 128), 1)
        tsb[...] = ts.astype(BF)
        tlb[...] = jnp.where(lane < NE, top, jnp.where(lane < 2 * NE, ts - top, 0.0)).astype(BF)

    def product(p, r):
        @pl.when(c == 0)
        def _():
            acc = dot_nt(pg[r, 0:HID], wu[0, lanes(p), :])
            acc += dot_nt(pg[r, HID : 2 * HID], wu[1, lanes(p), :])
            part[...] = acc + dot_nn(tsb[r, :], rt3[:, lanes(p)])

        @pl.when(c == 1)
        def _():
            acc = dot_nn(mr[r, 0:HID], wd[0, :, lanes(p)])
            part[...] = acc + dot_nn(mr[r, HID : 2 * HID], wd[1, :, lanes(p)])

    def tblock(hh, d, dist):
        return hh * NZ + zwrap(z + dist - 2 * d * dist)

    def sum_piece(d, far):
        return pl.ds(d * QUART, QUART) if far else pl.ds(0, HALF)

    def hop(st, d, t, far):
        rr = sum_piece(d, far)
        return rcopy(
            ring_s.at[st, d, t - 1, rr], ring_r.at[st, d, t - 1, rr], rs_ssem.at[st, d], rs_rsem.at[st, d, t - 1], znext(d)
        )

    def copy_rx(d, dist):
        return rcopy(xs.at[d, dist], xr.at[d, dist], rx_ssem.at[d, dist], rx_rsem.at[d, dist], partner)

    plane = [(dh, dq) for dh in range(2) for dq in range(NE) if dh or dq]

    def plane_dev(dh, dq):
        return lax.rem(h + dh, 2), qwrap(q + dq)

    def copy_g1(i, dh, dq):
        hh, qq = plane_dev(dh, dq)
        return rcopy(gp.at[hh * NE + qq], g1.at[i], g1_ssem.at[0], g1_rsem.at[0], dev(hh, z, c, qq))

    def copy_g2(dz):
        return rcopy(g2s, g2.at[dz], g2_ssem.at[0], g2_rsem.at[0], dev(h, zwrap(z + dz), c, q))

    me_p = h * NE + q

    def copy_g3(i, dh, dq):
        hh, qq = plane_dev(dh, dq)
        return rcopy(g3s, g3.at[:, lanes(me_p)], g3_ssem.at[0], g3_rsem.at[0], dev(hh, z, c, qq))

    all_g1 = rcopy(g1, g1, g1_ssem.at[0], g1_rsem.at[0], sib)
    near_g2 = g2.at[pl.ds(1, NZ - 1)]
    all_g2 = rcopy(near_g2, near_g2, g2_ssem.at[0], g2_rsem.at[0], sib)
    all_g3 = rcopy(g1, g1, g3_ssem.at[0], g3_rsem.at[0], sib)

    g4 = rcopy(g3, gr_ref, g4_sem.at[0], g4_sem.at[1], sib)
    g4_own = pltpu.make_async_copy(g3, gr_ref, g4_sem.at[2])

    def router_parts():
        tl = tlb[...]

        def one(p, carry):
            full = dot_tn(tl, gath[p])
            gp[p] = full[0:NE] + full[NE : 2 * NE]
            return carry

        lax.fori_loop(0, NBLK, one, 0)
        for i, (dh, dq) in enumerate(plane):
            copy_g1(i, dh, dq).start()

    def router_plane():
        all_g1.wait_recv()
        total = gp[me_p]
        for i in range(len(plane)):
            total = total + g1[i]
        g2s[...] = total
        for dz in range(1, NZ):
            copy_g2(dz).start()

    def router_column():
        all_g2.wait_recv()
        total = g2s[...]
        for dz in range(1, NZ):
            total = total + g2[dz]
        g3s[...] = total
        g3[:, lanes(me_p)] = total
        for i, (dh, dq) in enumerate(plane):
            copy_g3(i, dh, dq).start()

    def router_out():
        all_g3.wait_recv()
        g4.start()
        g4_own.start()

    gu_own = pltpu.make_async_copy(gu0, gu_ref, gsem.at[0])
    gd_own = pltpu.make_async_copy(gd0, gd_ref, gsem.at[0])
    gu_give = rcopy(gu, gu_ref, gsem.at[1], gsem.at[2], sib)
    gd_give = rcopy(gd, gd_ref, gsem.at[1], gsem.at[2], sib)

    def weight_grads(step):
        def one(p, carry):
            @pl.when(c == 0)
            def _():
                full = dot_tn(gath[p], pg[...]).astype(BF)
                gu0[lanes(p), :] = full[:, 0:HID]
                gu[lanes(p), :] = full[:, HID : 2 * HID]

            @pl.when(c == 1)
            def _():
                full = dot_tn(mr[...], gath[p]).astype(BF)
                gd[:, lanes(p)] = full[0:HID]
                gd0[:, lanes(p)] = full[HID : 2 * HID]

            return carry

        begin = jnp.where(step == 1, 0, jnp.where(step == FAR - 1, 4, 10))
        end = jnp.where(step == 1, 4, jnp.where(step == FAR - 1, 10, NBLK))

        @pl.when((step == 1) | (step == FAR - 1) | (step == FAR))
        def _():
            lax.fori_loop(begin, end, one, 0)

        @pl.when((step == FAR) & (c == 0))
        def _():
            gu_own.start()
            gu_give.start()

        @pl.when((step == FAR) & (c == 1))
        def _():
            gd_own.start()
            gd_give.start()

    def ret_copy(kind, dy):
        qd = group(kind == 0, dy)
        sems = r_ssem.at[kind], r_rsem.at[kind]
        if kind == 2:
            return rcopy(fs1.at[rows_of(lax.rem(qd, NY))], ret1.at[rows_of(y)], *sems, dev(1 - h, z, c, qd))
        return rcopy(fs0.at[rows_of(qd)], ret0.at[rows_of(q)], *sems, dev(h, z, c, qd))

    def ret_all(kind):
        ref = rows_in(fs0, kind)
        return rcopy(ref, ref, r_ssem.at[kind], r_rsem.at[kind], sib)

    last = FAR + 1

    def scatter_step(step, carry):
        nxt = FAR - step

        def share(d, carry2):
            @pl.when(((step == 0) & (d == 1)) | ((step >= 1) & (step < FAR)) | ((step == FAR) & (d == 0)))
            def _():
                product(tblock(1 - h, d, nxt), second())
                xs[d, nxt] = part[...].astype(BF)
                copy_rx(d, nxt).start()

            return carry2

        def stream(st, step):
            hh = 1 - h if st == 2 else h
            dist = last - step

            def one(d, carry2):
                @pl.when((((step == 1) | (step == last)) & (d == 0)) | ((step > 1) & (step < last)))
                def _():
                    product(tblock(hh, d, dist), second() if st == 0 else first())
                    total = part[...]
                    if st == 0:
                        far_d = jnp.where(step == 1, 1, d)
                        copy_rx(far_d, dist).wait_recv()
                        total = total + xr[far_d, dist].astype(F32)

                    @pl.when(step == 1)
                    def _():
                        for dd in range(2):
                            rr = slice(dd * QUART, (dd + 1) * QUART)
                            ring_s[st, dd, 0, rr] = total[rr].astype(BF)
                            hop(st, dd, 1, True).start()

                    @pl.when(step == 2)
                    def _():
                        hop(st, d, 1, True).wait_recv()
                        hop(st, d, 1, True).wait_send()
                        ring_s[st, d, 1] = total.astype(BF)
                        rr = pl.ds(d * QUART, QUART)
                        part[...] = total
                        got = part[rr, :] + ring_r[st, d, 0, rr, :].astype(F32)
                        ring_s[st, d, 1, rr, :] = got.astype(BF)
                        hop(st, d, 2, False).start()

                    @pl.when((step > 2) & (step < last))
                    def _():
                        hop(st, d, step - 1, False).wait_recv()
                        hop(st, d, step - 1, False).wait_send()
                        ring_s[st, d, step - 1] = (total + ring_r[st, d, step - 2].astype(F32)).astype(BF)
                        hop(st, d, step, False).start()

                    @pl.when(step == last)
                    def _():
                        hop(st, 0, FAR, False).wait_recv()
                        hop(st, 1, FAR, False).wait_recv()
                        got = total + ring_r[st, 0, FAR - 1].astype(F32) + ring_r[st, 1, FAR - 1].astype(F32)
                        if st == 2:
                            fs1[...] = got.astype(BF)
                        else:
                            fs0[second() if st == 0 else first(), :] = got.astype(BF)
                        for dy in range(NY):
                            if st == 0 and dy == 0:
                                ret0[rows_of(q), :] = fs0[rows_of(q), :]
                            else:
                                ret_copy(st, dy).start()

                return carry2

            lax.fori_loop(0, 2, one, 0)

        stream(1, step)

        @pl.when(step == FAR)
        def _():
            @pl.when(c == 0)
            def _():
                router_plane()

            stream(0, step - 1)

        stream(2, step)
        lax.fori_loop(0, 2, share, 0)
        stream(0, jnp.where(step < FAR, step - 1, step))

        @pl.when((step == 2) & (c == 0))
        def _():
            router_parts()

        @pl.when((step == FAR) & (c == 0))
        def _():
            router_column()

        weight_grads(step)
        return carry

    lax.fori_loop(0, last + 1, scatter_step, 0)

    for kind in (1, 2):
        ret_all(kind).wait_recv()
    got = dot_tn(pick[first(), :], ret0[first(), :]) + dot_tn(pick[first(), :], ret1[...])
    ret_all(0).wait_recv()
    got = got + dot_tn(pick[second(), :], ret0[second(), :])
    rounded = got.astype(BF)
    trade.wait_send()
    give[...] = dot_nt(rounded, place_other).astype(BF)
    give_tokens = rcopy(give, og_ref, o_sem.at[0], o_sem.at[1], sib)
    give_mixed = rcopy(give, om_ref, o_sem.at[0], o_sem.at[1], sib)
    put_tokens = pltpu.make_async_copy(keep, og_ref, o_sem.at[2])
    put_mixed = pltpu.make_async_copy(keep, om_ref, o_sem.at[2])

    @pl.when(c == 0)
    def _():
        give_tokens.start()

    @pl.when(c == 1)
    def _():
        give_mixed.start()

    keep[...] = dot_nt(rounded, place_mine).astype(BF)

    @pl.when(c == 0)
    def _():
        put_tokens.start()
        router_out()

    @pl.when(c == 1)
    def _():
        put_mixed.start()

    for kind in range(3):
        disp_all(kind).wait_send()
        ret_all(kind).wait_send()

    for d in range(2):
        for st in range(3):
            ring(st, d, FAR, True, 1).wait_send()
            hop(st, d, FAR, False).wait_send()
    copy_f(0, FAR - 1).wait_send()
    copy_f(1, FAR).wait_send()
    for k in range(FAR):
        copy_rx(0, k).wait_send()
        copy_rx(1, k + 1).wait_send()
    middle.wait_send()

    @pl.when(c == 0)
    def _():
        w_in_give.wait_send()
        meta_all.wait_send()
        all_g1.wait_send()
        all_g2.wait_send()
        all_g3.wait_send()
        g4.wait_send()
        g4_own.wait()
        gu_own.wait()
        gu_give.wait_send()
        gd_give.wait_recv()

    @pl.when(c == 1)
    def _():
        w_out_give.wait_send()
        g4.wait_recv()
        gd_own.wait()
        gd_give.wait_send()
        gu_give.wait_recv()

    @pl.when(c == 0)
    def _():
        put_tokens.wait()
        give_tokens.wait_send()
        give_mixed.wait_recv()

    @pl.when(c == 1)
    def _():
        put_mixed.wait()
        give_mixed.wait_send()
        give_tokens.wait_recv()


def vm(*shape, dtype=BF):
    return pltpu.VMEM(shape, dtype)


def dma(*shape):
    return pltpu.SemaphoreType.DMA(shape)


def store(om, og, gu, gd, gr, om_out, og_out, gu_out, gd_out, gr_out, sem):
    copies = [
        pltpu.make_async_copy(src, dst, sem.at[i])
        for i, (src, dst) in enumerate(((gu, gu_out), (gd, gd_out), (om, om_out), (og, og_out), (gr, gr_out)))
    ]
    for copy in copies:
        copy.start()
    for copy in copies:
        copy.wait()


def shards(tokens, expert_ids, slot_ids, router, up_weight, down_weight, cotangent):
    aspec = pl.BlockSpec(memory_space=pl.ANY)
    hspec = pl.BlockSpec(memory_space=pltpu.HBM)
    shapes = (
        jax.ShapeDtypeStruct((TOK, FEAT), BF),
        jax.ShapeDtypeStruct((TOK, FEAT), BF),
        jax.ShapeDtypeStruct((WIDTH, HID), BF),
        jax.ShapeDtypeStruct((HID, WIDTH), BF),
        jax.ShapeDtypeStruct((NE, WIDTH), F32),
    )
    results = pl.pallas_call(
        kernel,
        out_shape=(
            *shapes,
        ),
        in_specs=[hspec] * 7,
        out_specs=(aspec,) * 5,
        scratch_shapes=[
            vm(NBLK, ROWS, BLK), vm(2, WIDTH, HID), vm(2, HID, WIDTH), vm(WIDTH, HID), vm(HID, WIDTH), vm(WIDTH, HID), vm(HID, WIDTH),
            vm(128, WIDTH), vm(ROWS, TOK), vm(TOK, FEAT), vm(TOK, FEAT),
            vm(2, TOK, dtype=jnp.int32), vm(2, TOK, dtype=jnp.int32), vm(NE, WIDTH, dtype=F32),
            vm(TOK, FEAT), vm(ROWS, BLK), vm(ROWS, 128), vm(ROWS, 128),
            vm(ROWS, 2 * HID, dtype=F32), vm(ROWS, 128, dtype=F32), vm(ROWS, 2 * HID), vm(ROWS, 2 * HID),
            vm(ROWS, 2 * HID), vm(ROWS, 128), vm(ROWS, 128), vm(HALF, BLK, dtype=F32),
            vm(3, 2, FAR, HALF, BLK), vm(3, 2, FAR, HALF, BLK), vm(2, 5, HALF, BLK), vm(2, 5, HALF, BLK),
            vm(ROWS, BLK), vm(HALF, BLK), vm(ROWS, BLK), vm(HALF, BLK),
            vm(NBLK, NE, BLK, dtype=F32), vm(15, NE, BLK, dtype=F32), vm(NE, BLK, dtype=F32),
            vm(NZ, NE, BLK, dtype=F32), vm(NE, BLK, dtype=F32), vm(NE, WIDTH, dtype=F32),
            dma(4), dma(3), dma(2), dma(3), dma(3), dma(1), dma(1),
            dma(3, 2), dma(3, 2, FAR), dma(2), dma(2, 5), dma(2), dma(3, 2), dma(3, 2, FAR), dma(2, 5), dma(2, 5),
            dma(3), dma(3), dma(3), dma(3),
            dma(1), dma(1), dma(1), dma(1), dma(1), dma(1), dma(3),
        ],
        compiler_params=pltpu.CompilerParams(
            collective_id=0, has_side_effects=True, vmem_limit_bytes=47 << 20
        ),
    )(
        *(
            pltpu.with_memory_space_constraint(v, pltpu.HBM)
            for v in (tokens, cotangent, expert_ids.T, slot_ids.T, router.T, up_weight[0], down_weight[0])
        )
    )
    mixed, grad_tokens, gu, gd, gr = pl.pallas_call(
        store,
        out_shape=shapes,
        in_specs=[aspec] * 5,
        out_specs=(hspec,) * 5,
        scratch_shapes=[dma(5)],
        compiler_params=pltpu.CompilerParams(vmem_limit_bytes=1 << 20),
    )(*results)
    return (mixed, grad_tokens, gu[None], gd[None], gr.T)


def solution(mesh):
    in_specs = (
        P("expert", "section"),
        P("expert", None),
        P("expert", None),
        P(),
        P("expert", None, "section"),
        P("expert", "section", None),
        P("expert", "section"),
    )
    out_specs = (
        P("expert", "section"),
        P("expert", "section"),
        P("expert", None, "section"),
        P("expert", "section", None),
        P(),
    )
    return jax.shard_map(shards, mesh=mesh, in_specs=in_specs, out_specs=out_specs, check_vma=False)
```
